256 devices in a mesh: owner: 16 (over z, core), helper: 16 (over y, x).
Axes of the slice: x: 4, y: 4, z: 8, core: 2. Of those that a mesh axis runs over, the one named last changes fastest.
Arguments:
- points: bfloat16 [1024, 64, 512], P(('owner', 'helper')), may hold values from -1.5 to 1.5
- weights: bfloat16 [1024, 16, 512], P(('owner', 'helper')), may hold values from -6 to 6
- neighbours: int32 [1024, 48], P(('owner', 'helper')), may hold values from -1 to 1023, as said below
- counts: int32 [1024], P(('owner', 'helper')), may hold values from 1 to 48, as said below
Outputs:
- potential: float32 [1024, 16, 512], P(('owner', 'helper'))
The draws below stay inside these ranges and needn't reach their ends.
Inputs may be any that keep to these rules, and one draw needn't show every extreme that they name: `neighbours`: slot 0 of a leaf's list holds the leaf itself; slots 0 to counts - 1 hold distinct leaves, each in the same group of 64 consecutive leaves as the listed leaf or in the group just before or just after it; all other slots hold -1. `counts`: some leaf has a full list in every draw.
All inputs are finite; a program needn't handle non-finite values.
Results may differ from the reference program's by a relative error of at most 0.0028.
Values may be sent and summed in bfloat16 or wider, within the bound.
No kernel may reach another device: no remote copies, remote signals or barrier semaphores. Data moves between devices by JAX's collectives and lax.ppermute only.
A program may use at most 64 MiB of HBM per device.

```python
import jax
import jax.numpy as jnp
from jax import lax

DIM = 64
NV = 16
LEAF = 512
GROUP = 64
LEAVES = 1024
MAXNB = 48


def make_lists(key):
    base_key = jax.random.fold_in(key, 31)
    heavy_key, forced_key, light_key, score_key = jax.random.split(base_key, 4)
    leaf_ids = jnp.arange(LEAVES, dtype=jnp.int32)
    heavy = jax.random.randint(heavy_key, (LEAVES,), 0, 8) == 0
    forced = jax.random.randint(forced_key, (), 0, LEAVES)
    heavy = heavy | (leaf_ids == forced)
    light = jax.random.randint(light_key, (LEAVES,), 1, MAXNB // 4 + 1)
    sizes = jnp.where(heavy, MAXNB, light).astype(jnp.int32)
    offsets = jnp.arange(3 * GROUP, dtype=jnp.int32)
    starts = (leaf_ids // GROUP - 1) * GROUP
    candidates = starts[:, None] + offsets[None, :]
    usable = (candidates >= 0) & (candidates < LEAVES) & (candidates != leaf_ids[:, None])
    scores = jax.random.randint(score_key, (LEAVES, 3 * GROUP), 0, 1 << 20) * (3 * GROUP) + offsets[None, :]
    scores = jnp.where(usable, scores, -1)
    picked_scores, picked = lax.top_k(scores, MAXNB - 1)
    chosen = jnp.take_along_axis(candidates, picked, axis=1)
    lists = jnp.concatenate([leaf_ids[:, None], chosen], axis=1)
    slots = jnp.arange(MAXNB, dtype=jnp.int32)
    lists = jnp.where(slots[None, :] < sizes[:, None], lists, -1)
    return (lists.astype(jnp.int32), sizes)


def draw_neighbours(key, part):
    lists, sizes = make_lists(key)
    return lists


def draw_counts(key, part):
    lists, sizes = make_lists(key)
    return sizes


def block_scale(rng, dims, cuts, smallest, high):
    def one(dim, shards_of):
        heights = jax.random.uniform(jax.random.fold_in(jax.random.fold_in(rng, 6), dim), (shards_of,), jnp.float32, smallest / len(cuts), high / len(cuts))
        return jnp.repeat(jnp.exp(heights), dims[dim] // shards_of).reshape((-1,) + (1,) * (len(dims) - dim - 1))

    factor_of = one(*cuts[0])
    for cut in cuts[1:]:
        factor_of = factor_of * one(*cut)
    return factor_of


def noise(key, shape, spread, reach, shards=(), held_as=jnp.bfloat16):
    entries = jax.random.normal(key, shape, jnp.float32) * spread
    if len(shards) > 0:
        entries = block_scale(key, shape, shards, -0.22, 0.18) * entries
    return jnp.clip(entries, min=-reach, max=reach).astype(held_as)


def setup_inputs(seed: int = 0) -> dict:
    key_of = jax.random.split(jax.random.key(seed), 5)
    return {
        "points": noise(key_of[0], (LEAVES, DIM, LEAF), (2.0 / DIM ** 0.5), 1.5, ((0, 256),)),
        "weights": noise(key_of[1], (LEAVES, NV, LEAF), 1.0, 6.0, ((0, 256),)),
        "neighbours": draw_neighbours(jax.random.fold_in(key_of[4], 71), 0),
        "counts": draw_counts(jax.random.fold_in(key_of[4], 71), 0),
    }


def block_sum(target_points, target_norms, source_points, source_norms, source_weights):
    inner = lax.dot_general(source_points, target_points, (((0,), (0,)), ((), ())), preferred_element_type=jnp.float32)
    kernel = jnp.exp(inner - 0.5 * source_norms[:, None] - 0.5 * target_norms[None, :]).astype(jnp.bfloat16)
    return jnp.dot(source_weights, kernel, preferred_element_type=jnp.float32)


def reference(points, weights, neighbours, counts):
    widened = points.astype(jnp.float32)
    norms = jnp.einsum("ldp,ldp->lp", widened, widened)

    def one_leaf(leaf):
        def add_pair(slot, total):
            source = neighbours[leaf, slot]
            return total + block_sum(points[leaf], norms[leaf], points[source], norms[source], weights[source])

        start = jnp.zeros((weights.shape[1], points.shape[2]), jnp.float32)
        return lax.fori_loop(0, counts[leaf], add_pair, start)

    return lax.map(one_leaf, jnp.arange(points.shape[0], dtype=jnp.int32))
```

```python
import functools

import jax
import jax.numpy as jnp
from jax import lax
from jax.experimental import pallas as pl
from jax.experimental.pallas import tpu as pltpu
from jax.sharding import PartitionSpec as P

LOG2E = 1.4426950408889634
SIDE = 4
UNROLL = 4
CHUNK = 128
PRE = 128


def moved(value, step, along):
    pairs = []
    for h in range(SIDE * SIDE):
        r, c = divmod(h, SIDE)
        if along == 0:
            to = ((r + step) % SIDE) * SIDE + c
        else:
            to = r * SIDE + (c + step) % SIDE
        pairs.append((h, to))
    return lax.ppermute(value, "helper", pairs)


def nn(a, b):
    return lax.dot_general(
        a, b, (((1,), (0,)), ((), ())), preferred_element_type=jnp.float32
    )


def tn(a, b):
    return lax.dot_general(
        a, b, (((0,), (0,)), ((), ())), preferred_element_type=jnp.float32
    )


def list_kernel(
    local, me_ref, lists_ref, sizes_ref, own_ref, far_ref, count_ref
):
    first, row, column = me_ref[0], me_ref[1], me_ref[2]
    targets, _ = lists_ref.shape
    group = local * SIDE * SIDE
    dummy = targets << 16

    def per_target(t, carry):
        def entry(k, carry):
            own, far = carry
            s = lists_ref[t, k] - first
            g = s // group
            rest = s - g * group
            h = rest // local
            i = rest - h * local
            r = h // SIDE
            c = h - r * SIDE
            mine = c == column
            d = (row - r + SIDE) % SIDE
            block = d * local + i
            key = (t << 16) | (t << 8)
            own_ref[own] = key | block
            side = jnp.where(g == 0, 0, SIDE * local)
            far_ref[far] = key | (side + block)
            is_own = mine & (g == 1)
            is_far = mine & (g != 1)
            return (
                own + jnp.where(is_own, 1, 0),
                far + jnp.where(is_far, 1, 0),
            )

        return lax.fori_loop(0, sizes_ref[t, 0], entry, carry)

    own, far = lax.fori_loop(0, targets, per_target, (jnp.int32(0), jnp.int32(0)))
    count_ref[0] = own
    count_ref[1] = far
    for u in range(UNROLL + 2):
        own_ref[own + u] = dummy
        far_ref[far + u] = dummy


def three_pieces(n):
    high = n.astype(jnp.bfloat16).astype(jnp.float32)
    rest = n - high
    middle = rest.astype(jnp.bfloat16).astype(jnp.float32)
    return high, middle, rest - middle


def extra_rows(coords, source):
    wide = coords.astype(jnp.float32)
    n = jnp.sum(wide * wide, axis=0, keepdims=True)
    a, b, c = three_pieces(n)
    width = coords.shape[1]
    row = lax.broadcasted_iota(jnp.int32, (16, width), 0)
    one = jnp.float32(1.0) if source else jnp.float32(-0.5)
    scale = jnp.float32(1.0) if source else jnp.float32(-0.5)
    at = 0 if source else 3
    rows = jnp.where(row < 6, one, jnp.float32(0.0))
    for i, piece in enumerate((a, b, c)):
        rows = jnp.where(row == at + i, scale * piece, rows)
    return rows.astype(jnp.bfloat16)


def pair_kernel(
    n_sources, n_targets, with_start, which, count_ref, keys_ref, *refs
):
    source_refs, refs = refs[:n_sources], refs[n_sources:]
    target_refs, refs = refs[:n_targets], refs[n_targets:]
    if with_start:
        start_ref, refs = refs[0], refs[1:]
    out_ref, src, wts, tgt, acc, k0, k1, s0, s1 = refs
    local = source_refs[0].shape[0]
    dims = target_refs[0].shape[1]
    width = target_refs[0].shape[2]
    deep = dims + 16
    targets = n_targets * local
    kb, sb = (k0, k1), (s0, s1)

    for b, ref in enumerate(source_refs):
        for i in range(local):
            block = ref[i]
            src[b * local + i, :dims] = block[:dims]
            src[b * local + i, dims:] = extra_rows(block[:dims], True)
            wts[b * local + i] = block[dims:]
    for b, ref in enumerate(target_refs):
        for i in range(local):
            coords = ref[i]
            tgt[b * local + i, :dims] = coords
            tgt[b * local + i, dims:] = extra_rows(coords, False)
    if with_start:
        acc[:targets] = start_ref[...]
    else:
        acc[:targets] = jnp.zeros((targets,) + acc.shape[1:], jnp.float32)
    acc[targets] = jnp.zeros(acc.shape[1:], jnp.float32)
    k1[...] = jnp.zeros_like(k1)

    def picked(p):
        key = keys_ref[p]
        return key & 255, (key >> 8) & 255, key >> 16

    def exponent(s, lo, hi, rows):
        return tn(src[s, :, lo:hi], rows)

    def ahead(p, buffer):
        s, t, _ = picked(p)
        rows = tgt[t]
        for i in range(0, PRE, CHUNK):
            buffer[i : i + CHUNK] = exponent(s, i, i + CHUNK, rows)

    def gauss(e):
        return jnp.exp2(e * LOG2E).astype(jnp.bfloat16)

    def step(p, k_in, k_out, s_now, s_next):
        s, t, _ = picked(p)
        rows = tgt[t]
        for i in range(0, PRE, CHUNK):
            k_out[i : i + CHUNK] = gauss(s_now[i : i + CHUNK])
        for i in range(PRE, width, CHUNK):
            k_out[i : i + CHUNK] = gauss(exponent(s, i, i + CHUNK, rows))
        ahead(p + 1, s_next)
        s_last, _, a_last = picked(jnp.maximum(p - 1, 0))
        acc[a_last] += nn(wts[s_last], k_in[...])

    ahead(0, s0)

    def body(h, carry):
        for u in range(UNROLL):
            step(
                UNROLL * h + u,
                kb[(u + 1) % 2],
                kb[u % 2],
                sb[u % 2],
                sb[(u + 1) % 2],
            )
        return carry

    lax.fori_loop(0, (count_ref[which] + UNROLL) // UNROLL, body, 0)
    out_ref[...] = acc[:targets]


def pair_sums(which, count, keys, sources, targets, start=None):
    local, rows, width = sources[0].shape
    dims = targets[0].shape[1]
    vectors = rows - dims
    n_src, n_tgt = len(sources) * local, len(targets) * local
    smem = pl.BlockSpec(memory_space=pltpu.SMEM)
    vmem = pl.BlockSpec(memory_space=pltpu.VMEM)
    more = () if start is None else (start,)
    pairs = 40
    return pl.pallas_call(
        functools.partial(
            pair_kernel, len(sources), len(targets), start is not None, which
        ),
        out_shape=jax.ShapeDtypeStruct((n_tgt, vectors, width), jnp.float32),
        in_specs=[smem, smem] + [vmem] * (len(sources) + len(targets) + len(more)),
        out_specs=vmem,
        scratch_shapes=[
            pltpu.VMEM((n_src, dims + 16, width), jnp.bfloat16),
            pltpu.VMEM((n_src, vectors, width), jnp.bfloat16),
            pltpu.VMEM((n_tgt, dims + 16, width), jnp.bfloat16),
            pltpu.VMEM((n_tgt + 1, vectors, width), jnp.float32),
            pltpu.VMEM((width, width), jnp.bfloat16),
            pltpu.VMEM((width, width), jnp.bfloat16),
            pltpu.VMEM((PRE, width), jnp.float32),
            pltpu.VMEM((PRE, width), jnp.float32),
        ],
        compiler_params=pltpu.CompilerParams(vmem_limit_bytes=28 << 20),
        cost_estimate=pl.CostEstimate(
            flops=2 * pairs * width * width * rows,
            transcendentals=pairs * width * width,
            bytes_accessed=(n_src * rows + n_tgt * dims) * width * 2,
        ),
        name="pairs_own" if start is None else "pairs_far",
    )(count, keys, *sources, *targets, *more)


def on_device(points, weights, neighbours, counts):
    local, dims, width = points.shape
    slots = neighbours.shape[1]
    helpers = lax.axis_size("helper")
    owners = lax.axis_size("owner")
    group = local * helpers
    helper = lax.axis_index("helper")
    first_leaf = (lax.axis_index("owner") - 1) * group
    up = [(i, i + 1) for i in range(owners - 1)]
    down = [(j, i) for i, j in up]

    small = jnp.concatenate([neighbours, counts[:, None]], axis=1)
    blocks = jnp.concatenate([points, weights], axis=1)

    smalls = [small] + [moved(small, d, 1) for d in range(1, SIDE)]
    order = (1, 3, 2)
    column = {0: blocks}
    for d in order:
        column[d] = moved(blocks, d, 0)
    row = {0: points}
    for d in order:
        row[d] = moved(points, d, 1)
    before, after = {}, {}
    for d in (0,) + order:
        before[d] = lax.ppermute(column[d], "owner", up)
        after[d] = lax.ppermute(column[d], "owner", down)

    lists = jnp.concatenate(smalls, axis=0)
    me = jnp.stack([first_leaf, helper // SIDE, helper % SIDE]).astype(jnp.int32)
    smem = pl.BlockSpec(memory_space=pltpu.SMEM)
    room = SIDE * local * slots + 8
    own, far, count = pl.pallas_call(
        functools.partial(list_kernel, local),
        out_shape=(
            jax.ShapeDtypeStruct((room,), jnp.int32),
            jax.ShapeDtypeStruct((room,), jnp.int32),
            jax.ShapeDtypeStruct((2,), jnp.int32),
        ),
        in_specs=[smem] * 3,
        out_specs=(smem,) * 3,
        name="pair_lists",
    )(me, lists[:, :slots], lists[:, slots:])

    targets = [row[d] for d in range(SIDE)]
    total = pair_sums(0, count, own, [column[d] for d in range(SIDE)], targets)
    total = pair_sums(
        1,
        count,
        far,
        [before[d] for d in range(SIDE)] + [after[d] for d in range(SIDE)],
        targets,
        total,
    )
    parts = total.reshape(SIDE, local, *total.shape[1:])
    result = parts[0]
    for d in range(1, SIDE):
        result = result + moved(parts[d], -d, 1)
    return result


def solution(mesh):
    placed = (
        P(("owner", "helper"), None, None),
        P(("owner", "helper"), None, None),
        P(("owner", "helper"), None),
        P(("owner", "helper")),
    )
    return jax.shard_map(
        on_device,
        mesh=mesh,
        in_specs=placed,
        out_specs=P(("owner", "helper"), None, None),
        check_vma=False,
    )
```

```python
import functools

import jax
import jax.numpy as jnp
from jax import lax
from jax.experimental import pallas as pl
from jax.experimental.pallas import tpu as pltpu
from jax.sharding import PartitionSpec as P

LOG2E = 1.4426950408889634
SIDE = 4
UNROLL = 4
CHUNK = 128
PRE = 128


def moved(value, step, along):
    pairs = []
    for h in range(SIDE * SIDE):
        r, c = divmod(h, SIDE)
        if along == 0:
            to = ((r + step) % SIDE) * SIDE + c
        else:
            to = r * SIDE + (c + step) % SIDE
        pairs.append((h, to))
    return lax.ppermute(value, "helper", pairs)


def nn(a, b):
    return lax.dot_general(
        a, b, (((1,), (0,)), ((), ())), preferred_element_type=jnp.float32
    )


def tn(a, b):
    return lax.dot_general(
        a, b, (((0,), (0,)), ((), ())), preferred_element_type=jnp.float32
    )


def list_kernel(sizes_ref, keys_ref, own_ref, far_ref, count_ref):
    targets, _ = keys_ref.shape
    dummy = targets << 16

    def per_target(t, carry):
        def entry(k, carry):
            own, far = carry
            key = keys_ref[t, k]
            kind = key >> 24
            own_ref[own] = key & 0xFFFFFF
            far_ref[far] = key & 0xFFFFFF
            return (
                own + jnp.where(kind == 0, 1, 0),
                far + jnp.where(kind == 1, 1, 0),
            )

        return lax.fori_loop(0, sizes_ref[t, 0], entry, carry)

    own, far = lax.fori_loop(0, targets, per_target, (jnp.int32(0), jnp.int32(0)))
    count_ref[0] = own
    count_ref[1] = far
    for u in range(UNROLL + 2):
        own_ref[own + u] = dummy
        far_ref[far + u] = dummy


def keys_of(lists, first, row, column, local):
    rest = lists - first
    g = rest // (local * SIDE * SIDE)
    place = rest % (local * SIDE * SIDE)
    h, i = place // local, place % local
    r, c = h // SIDE, h % SIDE
    block = (row - r + SIDE) % SIDE * local + i
    slot = block + jnp.where(g == 2, SIDE * local, 0)
    kind = jnp.where(c == column, jnp.where(g == 1, 0, 1), 2)
    t = lax.broadcasted_iota(jnp.int32, lists.shape, 0)
    return (kind << 24) | (t << 16) | (t << 8) | slot


def three_pieces(n):
    high = n.astype(jnp.bfloat16).astype(jnp.float32)
    rest = n - high
    middle = rest.astype(jnp.bfloat16).astype(jnp.float32)
    return high, middle, rest - middle


def extra_rows(coords, source):
    wide = coords.astype(jnp.float32)
    n = jnp.sum(wide * wide, axis=0, keepdims=True)
    a, b, c = three_pieces(n)
    width = coords.shape[1]
    row = lax.broadcasted_iota(jnp.int32, (16, width), 0)
    one = jnp.float32(1.0) if source else jnp.float32(-0.5)
    scale = jnp.float32(1.0) if source else jnp.float32(-0.5)
    at = 0 if source else 3
    rows = jnp.where(row < 6, one, jnp.float32(0.0))
    for i, piece in enumerate((a, b, c)):
        rows = jnp.where(row == at + i, scale * piece, rows)
    return rows.astype(jnp.bfloat16)


def pair_kernel(
    n_sources, n_targets, with_start, which, count_ref, keys_ref, *refs
):
    source_refs, refs = refs[:n_sources], refs[n_sources:]
    target_refs, refs = refs[:n_targets], refs[n_targets:]
    if with_start:
        start_ref, refs = refs[0], refs[1:]
    out_ref, src, wts, tgt, acc, k0, k1, s0, s1 = refs
    local = source_refs[0].shape[0]
    dims = target_refs[0].shape[1]
    width = target_refs[0].shape[2]
    deep = dims + 16
    targets = n_targets * local
    kb, sb = (k0, k1), (s0, s1)

    for b, ref in enumerate(source_refs):
        for i in range(local):
            block = ref[i]
            src[b * local + i, :dims] = block[:dims]
            src[b * local + i, dims:] = extra_rows(block[:dims], True)
            wts[b * local + i] = block[dims:]
    for b, ref in enumerate(target_refs):
        for i in range(local):
            coords = ref[i]
            tgt[b * local + i, :dims] = coords
            tgt[b * local + i, dims:] = extra_rows(coords, False)
    if with_start:
        acc[:targets] = start_ref[...]
    else:
        acc[:targets] = jnp.zeros((targets,) + acc.shape[1:], jnp.float32)
    acc[targets] = jnp.zeros(acc.shape[1:], jnp.float32)
    k1[...] = jnp.zeros_like(k1)

    def picked(p):
        key = keys_ref[p]
        return key & 255, (key >> 8) & 255, key >> 16

    def exponent(s, lo, hi, rows):
        return tn(src[s, :, lo:hi], rows)

    def ahead(p, buffer):
        s, t, _ = picked(p)
        rows = tgt[t]
        for i in range(0, PRE, CHUNK):
            buffer[i : i + CHUNK] = exponent(s, i, i + CHUNK, rows)

    def gauss(e):
        return jnp.exp2(e * LOG2E).astype(jnp.bfloat16)

    def step(p, k_in, k_out, s_now, s_next):
        s, t, _ = picked(p)
        rows = tgt[t]
        for i in range(0, PRE, CHUNK):
            k_out[i : i + CHUNK] = gauss(s_now[i : i + CHUNK])
        for i in range(PRE, width, CHUNK):
            k_out[i : i + CHUNK] = gauss(exponent(s, i, i + CHUNK, rows))
        ahead(p + 1, s_next)
        s_last, _, a_last = picked(jnp.maximum(p - 1, 0))
        acc[a_last] += nn(wts[s_last], k_in[...])

    ahead(0, s0)

    def body(h, carry):
        for u in range(UNROLL):
            step(
                UNROLL * h + u,
                kb[(u + 1) % 2],
                kb[u % 2],
                sb[u % 2],
                sb[(u + 1) % 2],
            )
        return carry

    lax.fori_loop(0, (count_ref[which] + UNROLL) // UNROLL, body, 0)
    out_ref[...] = acc[:targets]


def pair_sums(which, count, keys, sources, targets, start=None):
    local, rows, width = sources[0].shape
    dims = targets[0].shape[1]
    vectors = rows - dims
    n_src, n_tgt = len(sources) * local, len(targets) * local
    smem = pl.BlockSpec(memory_space=pltpu.SMEM)
    vmem = pl.BlockSpec(memory_space=pltpu.VMEM)
    more = () if start is None else (start,)
    pairs = 40
    return pl.pallas_call(
        functools.partial(
            pair_kernel, len(sources), len(targets), start is not None, which
        ),
        out_shape=jax.ShapeDtypeStruct((n_tgt, vectors, width), jnp.float32),
        in_specs=[smem, smem] + [vmem] * (len(sources) + len(targets) + len(more)),
        out_specs=vmem,
        scratch_shapes=[
            pltpu.VMEM((n_src, dims + 16, width), jnp.bfloat16),
            pltpu.VMEM((n_src, vectors, width), jnp.bfloat16),
            pltpu.VMEM((n_tgt, dims + 16, width), jnp.bfloat16),
            pltpu.VMEM((n_tgt + 1, vectors, width), jnp.float32),
            pltpu.VMEM((width, width), jnp.bfloat16),
            pltpu.VMEM((width, width), jnp.bfloat16),
            pltpu.VMEM((PRE, width), jnp.float32),
            pltpu.VMEM((PRE, width), jnp.float32),
        ],
        compiler_params=pltpu.CompilerParams(vmem_limit_bytes=28 << 20),
        cost_estimate=pl.CostEstimate(
            flops=2 * pairs * width * width * rows,
            transcendentals=pairs * width * width,
            bytes_accessed=(n_src * rows + n_tgt * dims) * width * 2,
        ),
        name="pairs_own" if start is None else "pairs_far",
    )(count, keys, *sources, *targets, *more)


def on_device(points, weights, neighbours, counts):
    local, dims, width = points.shape
    slots = neighbours.shape[1]
    helpers = lax.axis_size("helper")
    owners = lax.axis_size("owner")
    group = local * helpers
    helper = lax.axis_index("helper")
    first_leaf = (lax.axis_index("owner") - 1) * group
    up = [(i, i + 1) for i in range(owners - 1)]
    down = [(j, i) for i, j in up]

    small = jnp.concatenate([neighbours, counts[:, None]], axis=1)
    blocks = jnp.concatenate([points, weights], axis=1)

    smalls = [small] + [moved(small, d, 1) for d in range(1, SIDE)]
    order = (1, 3, 2)
    column = {0: blocks}
    for d in order:
        column[d] = moved(blocks, d, 0)
    row = {0: points}
    for d in order:
        row[d] = moved(points, d, 1)
    before, after = {}, {}
    for d in (0,) + order:
        before[d] = lax.ppermute(column[d], "owner", up)
        after[d] = lax.ppermute(column[d], "owner", down)

    lists = jnp.concatenate(smalls, axis=0)
    keys = keys_of(lists[:, :slots], first_leaf, helper // SIDE, helper % SIDE, local)
    smem = pl.BlockSpec(memory_space=pltpu.SMEM)
    room = SIDE * local * slots + 8
    own, far, count = pl.pallas_call(
        list_kernel,
        out_shape=(
            jax.ShapeDtypeStruct((room,), jnp.int32),
            jax.ShapeDtypeStruct((room,), jnp.int32),
            jax.ShapeDtypeStruct((2,), jnp.int32),
        ),
        in_specs=[smem] * 2,
        out_specs=(smem,) * 3,
        name="pair_lists",
    )(lists[:, slots:], keys)

    targets = [row[d] for d in range(SIDE)]
    total = pair_sums(0, count, own, [column[d] for d in range(SIDE)], targets)
    total = pair_sums(
        1,
        count,
        far,
        [before[d] for d in range(SIDE)] + [after[d] for d in range(SIDE)],
        targets,
        total,
    )
    parts = total.reshape(SIDE, local, *total.shape[1:])
    result = parts[0]
    for d in range(1, SIDE):
        result = result + moved(parts[d], -d, 1)
    return result


def solution(mesh):
    placed = (
        P(("owner", "helper"), None, None),
        P(("owner", "helper"), None, None),
        P(("owner", "helper"), None),
        P(("owner", "helper")),
    )
    return jax.shard_map(
        on_device,
        mesh=mesh,
        in_specs=placed,
        out_specs=P(("owner", "helper"), None, None),
        check_vma=False,
    )
```

```python
import functools

import jax
import jax.numpy as jnp
from jax import lax
from jax.experimental import pallas as pl
from jax.experimental.pallas import tpu as pltpu
from jax.sharding import PartitionSpec as P

LOG2E = 1.4426950408889634
SIDE = 4
UNROLL = 4
CHUNK = 128
PRE = 128
AT_ONCE = 4


def moved(value, step, along):
    pairs = []
    for h in range(SIDE * SIDE):
        r, c = divmod(h, SIDE)
        if along == 0:
            to = ((r + step) % SIDE) * SIDE + c
        else:
            to = r * SIDE + (c + step) % SIDE
        pairs.append((h, to))
    return lax.ppermute(value, "helper", pairs)


def nn(a, b):
    return lax.dot_general(
        a, b, (((1,), (0,)), ((), ())), preferred_element_type=jnp.float32
    )


def tn(a, b):
    return lax.dot_general(
        a, b, (((0,), (0,)), ((), ())), preferred_element_type=jnp.float32
    )


def list_kernel(sizes_ref, keys_ref, own_ref, far_ref, count_ref):
    targets, _ = keys_ref.shape
    dummy = targets << 16

    def per_target(t, carry):
        def some(q, carry):
            own, far = carry
            for u in range(AT_ONCE):
                key = keys_ref[t, AT_ONCE * q + u]
                kind = key >> 24
                own_ref[own] = key & 0xFFFFFF
                far_ref[far] = key & 0xFFFFFF
                own = own + jnp.where(kind == 0, 1, 0)
                far = far + jnp.where(kind == 1, 1, 0)
            return own, far

        return lax.fori_loop(0, (sizes_ref[t, 0] + AT_ONCE - 1) // AT_ONCE, some, carry)

    own, far = lax.fori_loop(0, targets, per_target, (jnp.int32(0), jnp.int32(0)))
    count_ref[0] = own
    count_ref[1] = far
    for u in range(UNROLL + 2):
        own_ref[own + u] = dummy
        far_ref[far + u] = dummy


def keys_of(lists, sizes, first, row, column, local):
    rest = lists - first
    g = rest // (local * SIDE * SIDE)
    place = rest % (local * SIDE * SIDE)
    h, i = place // local, place % local
    r, c = h // SIDE, h % SIDE
    block = (row - r + SIDE) % SIDE * local + i
    used = lax.broadcasted_iota(jnp.int32, lists.shape, 1) < sizes
    slot = jnp.where(used, block + jnp.where(g == 2, SIDE * local, 0), 0)
    kind = jnp.where(used & (c == column), jnp.where(g == 1, 0, 1), 2)
    t = lax.broadcasted_iota(jnp.int32, lists.shape, 0)
    return (kind << 24) | (t << 16) | (t << 8) | slot


def three_pieces(n):
    high = n.astype(jnp.bfloat16).astype(jnp.float32)
    rest = n - high
    middle = rest.astype(jnp.bfloat16).astype(jnp.float32)
    return high, middle, rest - middle


def extra_rows(coords, source):
    wide = coords.astype(jnp.float32)
    n = jnp.sum(wide * wide, axis=0, keepdims=True)
    a, b, c = three_pieces(n)
    width = coords.shape[1]
    row = lax.broadcasted_iota(jnp.int32, (16, width), 0)
    one = jnp.float32(1.0) if source else jnp.float32(-0.5)
    scale = jnp.float32(1.0) if source else jnp.float32(-0.5)
    at = 0 if source else 3
    rows = jnp.where(row < 6, one, jnp.float32(0.0))
    for i, piece in enumerate((a, b, c)):
        rows = jnp.where(row == at + i, scale * piece, rows)
    return rows.astype(jnp.bfloat16)


def pair_kernel(
    n_sources, n_targets, with_start, which, count_ref, keys_ref, *refs
):
    source_refs, refs = refs[:n_sources], refs[n_sources:]
    target_refs, refs = refs[:n_targets], refs[n_targets:]
    if with_start:
        start_ref, refs = refs[0], refs[1:]
    out_ref, src, wts, tgt, acc, k0, k1, s0, s1 = refs
    local = source_refs[0].shape[0]
    dims = target_refs[0].shape[1]
    width = target_refs[0].shape[2]
    deep = dims + 16
    targets = n_targets * local
    kb, sb = (k0, k1), (s0, s1)

    for b, ref in enumerate(source_refs):
        for i in range(local):
            block = ref[i]
            src[b * local + i, :dims] = block[:dims]
            src[b * local + i, dims:] = extra_rows(block[:dims], True)
            wts[b * local + i] = block[dims:]
    for b, ref in enumerate(target_refs):
        for i in range(local):
            coords = ref[i]
            tgt[b * local + i, :dims] = coords
            tgt[b * local + i, dims:] = extra_rows(coords, False)
    if with_start:
        acc[:targets] = start_ref[...]
    else:
        acc[:targets] = jnp.zeros((targets,) + acc.shape[1:], jnp.float32)
    acc[targets] = jnp.zeros(acc.shape[1:], jnp.float32)
    k1[...] = jnp.zeros_like(k1)

    def picked(p):
        key = keys_ref[p]
        return key & 255, (key >> 8) & 255, key >> 16

    def exponent(s, lo, hi, rows):
        return tn(src[s, :, lo:hi], rows)

    def ahead(p, buffer):
        s, t, _ = picked(p)
        rows = tgt[t]
        for i in range(0, PRE, CHUNK):
            buffer[i : i + CHUNK] = exponent(s, i, i + CHUNK, rows)

    def gauss(e):
        return jnp.exp2(e * LOG2E).astype(jnp.bfloat16)

    def step(p, k_in, k_out, s_now, s_next):
        s, t, _ = picked(p)
        rows = tgt[t]
        for i in range(0, PRE, CHUNK):
            k_out[i : i + CHUNK] = gauss(s_now[i : i + CHUNK])
        for i in range(PRE, width, CHUNK):
            k_out[i : i + CHUNK] = gauss(exponent(s, i, i + CHUNK, rows))
        ahead(p + 1, s_next)
        s_last, _, a_last = picked(jnp.maximum(p - 1, 0))
        acc[a_last] += nn(wts[s_last], k_in[...])

    ahead(0, s0)

    def body(h, carry):
        for u in range(UNROLL):
            step(
                UNROLL * h + u,
                kb[(u + 1) % 2],
                kb[u % 2],
                sb[u % 2],
                sb[(u + 1) % 2],
            )
        return carry

    lax.fori_loop(0, (count_ref[which] + UNROLL) // UNROLL, body, 0)
    out_ref[...] = acc[:targets]


def pair_sums(which, count, keys, sources, targets, start=None):
    local, rows, width = sources[0].shape
    dims = targets[0].shape[1]
    vectors = rows - dims
    n_src, n_tgt = len(sources) * local, len(targets) * local
    smem = pl.BlockSpec(memory_space=pltpu.SMEM)
    vmem = pl.BlockSpec(memory_space=pltpu.VMEM)
    more = () if start is None else (start,)
    pairs = 40
    return pl.pallas_call(
        functools.partial(
            pair_kernel, len(sources), len(targets), start is not None, which
        ),
        out_shape=jax.ShapeDtypeStruct((n_tgt, vectors, width), jnp.float32),
        in_specs=[smem, smem] + [vmem] * (len(sources) + len(targets) + len(more)),
        out_specs=vmem,
        scratch_shapes=[
            pltpu.VMEM((n_src, dims + 16, width), jnp.bfloat16),
            pltpu.VMEM((n_src, vectors, width), jnp.bfloat16),
            pltpu.VMEM((n_tgt, dims + 16, width), jnp.bfloat16),
            pltpu.VMEM((n_tgt + 1, vectors, width), jnp.float32),
            pltpu.VMEM((width, width), jnp.bfloat16),
            pltpu.VMEM((width, width), jnp.bfloat16),
            pltpu.VMEM((PRE, width), jnp.float32),
            pltpu.VMEM((PRE, width), jnp.float32),
        ],
        compiler_params=pltpu.CompilerParams(vmem_limit_bytes=28 << 20),
        cost_estimate=pl.CostEstimate(
            flops=2 * pairs * width * width * rows,
            transcendentals=pairs * width * width,
            bytes_accessed=(n_src * rows + n_tgt * dims) * width * 2,
        ),
        name="pairs_own" if start is None else "pairs_far",
    )(count, keys, *sources, *targets, *more)


def on_device(points, weights, neighbours, counts):
    local, dims, width = points.shape
    slots = neighbours.shape[1]
    helpers = lax.axis_size("helper")
    owners = lax.axis_size("owner")
    group = local * helpers
    helper = lax.axis_index("helper")
    first_leaf = (lax.axis_index("owner") - 1) * group
    up = [(i, (i + 1) % owners) for i in range(owners)]
    down = [(j, i) for i, j in up]

    small = jnp.concatenate([neighbours, counts[:, None]], axis=1)
    blocks = jnp.concatenate([points, weights], axis=1)

    smalls = [small] + [moved(small, d, 1) for d in range(1, SIDE)]
    order = (1, 3, 2)
    column = {0: blocks}
    for d in order:
        column[d] = moved(blocks, d, 0)
    row = {0: points}
    for d in order:
        row[d] = moved(points, d, 1)
    lists = jnp.concatenate(smalls, axis=0)
    keys = keys_of(lists[:, :slots], lists[:, slots:], first_leaf, helper // SIDE, helper % SIDE, local)
    smem = pl.BlockSpec(memory_space=pltpu.SMEM)
    room = SIDE * local * slots + 8
    own, far, count = pl.pallas_call(
        list_kernel,
        out_shape=(
            jax.ShapeDtypeStruct((room,), jnp.int32),
            jax.ShapeDtypeStruct((room,), jnp.int32),
            jax.ShapeDtypeStruct((2,), jnp.int32),
        ),
        in_specs=[smem] * 2,
        out_specs=(smem,) * 3,
        name="pair_lists",
    )(lists[:, slots:], keys)

    before, after = {}, {}
    for d in (0,) + order:
        block = column[d]
        if d == order[-1]:
            block, own, far, count = lax.optimization_barrier((block, own, far, count))
            column[d] = block
        before[d] = lax.ppermute(block, "owner", up)
        after[d] = lax.ppermute(block, "owner", down)

    targets = [row[d] for d in range(SIDE)]
    total = pair_sums(0, count, own, [column[d] for d in range(SIDE)], targets)
    total = pair_sums(
        1,
        count,
        far,
        [before[d] for d in range(SIDE)] + [after[d] for d in range(SIDE)],
        targets,
        total,
    )
    parts = total.reshape(SIDE, local, *total.shape[1:])
    result = parts[0]
    for d in range(1, SIDE):
        result = result + moved(parts[d], -d, 1)
    return result


def solution(mesh):
    placed = (
        P(("owner", "helper"), None, None),
        P(("owner", "helper"), None, None),
        P(("owner", "helper"), None),
        P(("owner", "helper")),
    )
    return jax.shard_map(
        on_device,
        mesh=mesh,
        in_specs=placed,
        out_specs=P(("owner", "helper"), None, None),
        check_vma=False,
    )
```

```python
import functools

import jax
import jax.numpy as jnp
from jax import lax
from jax.experimental import pallas as pl
from jax.experimental.pallas import tpu as pltpu
from jax.sharding import PartitionSpec as P


LOG2E = 1.4426950408889634
SIDE = 4
LOCAL = 4
GROUP = LOCAL * SIDE * SIDE
UNROLL = 4
CHUNK = 128
PRE = 128
AT_ONCE = 4
TILE = 16
LISTS = 12
UNUSED = 255


def moved(value, step, along):
    pairs = []
    for h in range(SIDE * SIDE):
        r, c = divmod(h, SIDE)
        if along == 0:
            to = ((r + step) % SIDE) * SIDE + c
        else:
            to = r * SIDE + (c + step) % SIDE
        pairs.append((h, to))
    return lax.ppermute(value, "helper", pairs)


def nn(a, b):
    return lax.dot_general(
        a, b, (((1,), (0,)), ((), ())), preferred_element_type=jnp.float32
    )


def tn(a, b):
    return lax.dot_general(
        a, b, (((0,), (0,)), ((), ())), preferred_element_type=jnp.float32
    )


def pack_kernel(first_ref, points, weights, lists, counts, s_out, t_out, tile):
    dims = points.shape[1]
    slots = lists.shape[1]
    top = LOCAL * dims
    for i in range(LOCAL):
        coords = points[i]
        s_out[i * dims : (i + 1) * dims] = coords
        t_out[i * dims : (i + 1) * dims] = coords
        wide = coords.astype(jnp.float32)
        n = jnp.sum(wide * wide, axis=0, keepdims=True)
        high = n.astype(jnp.bfloat16).astype(jnp.float32)
        rest = n - high
        middle = rest.astype(jnp.bfloat16).astype(jnp.float32)
        tile[3 * i : 3 * i + 1] = high
        tile[3 * i + 1 : 3 * i + 2] = middle
        tile[3 * i + 2 : 3 * i + 3] = rest - middle
        at = top + TILE + i * weights.shape[1]
        s_out[at : at + weights.shape[1]] = weights[i]
    tile[LISTS : LISTS + 3] = jnp.ones((3, tile.shape[1]), jnp.float32)
    tile[LISTS + 3 :] = jnp.zeros((1, tile.shape[1]), jnp.float32)
    s_out[top : top + TILE] = tile[...].astype(jnp.bfloat16)
    tile[LISTS:] = jnp.zeros((LOCAL, tile.shape[1]), jnp.float32)
    slot = lax.broadcasted_iota(jnp.int32, (LOCAL, slots), 1)
    size = counts[...]
    near = jnp.where(slot < size, lists[...] - first_ref[0], UNUSED)
    tile[LISTS:, :slots] = near.astype(jnp.float32)
    tile[LISTS:, slots : slots + 1] = size.astype(jnp.float32)
    t_out[top:] = tile[...].astype(jnp.bfloat16)


def target_kernel(slots, me_ref, *refs):
    blocks, refs = refs[:SIDE], refs[SIDE:]
    tgt, own_ref, far_ref, count_ref, tile, norm, keys, keys_s, sem = refs
    dims = tgt.shape[1] - TILE
    top = LOCAL * dims
    norm[...] = jnp.zeros_like(norm)
    for b, ref in enumerate(blocks):
        tile[...] = ref[top:].astype(jnp.float32)
        keys[b * LOCAL : (b + 1) * LOCAL] = tile[LISTS:, :128].astype(jnp.int32)
    s = keys[...]
    g, h, i = s >> 6, (s >> 2) & 15, s & 3
    used = s < UNUSED
    lane = lax.broadcasted_iota(jnp.int32, s.shape, 1)
    t = lax.broadcasted_iota(jnp.int32, s.shape, 0)
    block = ((me_ref[0] - (h >> 2)) & 3) * LOCAL + i
    slot = jnp.where(used, block + jnp.where(g == 2, SIDE * LOCAL, 0), 0)
    mine = used & ((h & 3) == me_ref[1])
    kind = jnp.where(mine, jnp.where(g == 1, 0, 1), 2)
    key = (kind << 24) | (t << 16) | (t << 8) | slot
    keys[...] = jnp.where(lane == slots, s, key)
    copy = pltpu.make_async_copy(keys, keys_s, sem)
    copy.start()
    for b, ref in enumerate(blocks):
        tile[...] = ref[top:].astype(jnp.float32)
        for j in range(LOCAL):
            tgt[b * LOCAL + j, :dims] = ref[j * dims : (j + 1) * dims]
            norm[LISTS : LISTS + 3] = -0.5 * tile[3 * j : 3 * j + 3]
            tgt[b * LOCAL + j, dims:] = norm[...].astype(jnp.bfloat16)
    copy.wait()

    def per_target(t, carry):
        def some(q, carry):
            own, far = carry
            for u in range(AT_ONCE):
                key = keys_s[t, AT_ONCE * q + u]
                kind = key >> 24
                own_ref[own] = key & 0xFFFFFF
                far_ref[far] = key & 0xFFFFFF
                own = own + jnp.where(kind == 0, 1, 0)
                far = far + jnp.where(kind == 1, 1, 0)
            return own, far

        turns = (keys_s[t, slots] + (AT_ONCE - 1)) >> 2
        return lax.fori_loop(0, turns, some, carry)

    targets = SIDE * LOCAL
    own, far = lax.fori_loop(0, targets, per_target, (jnp.int32(0), jnp.int32(0)))
    count_ref[0] = own
    count_ref[1] = far
    for u in range(UNROLL + 2):
        own_ref[own + u] = jnp.int32(targets << 16)
        far_ref[far + u] = jnp.int32(targets << 16)


def pair_kernel(which, places, last, count_ref, keys_ref, *refs):
    n_refs = 1 + max(p[0] for p in places)
    source_refs, refs = refs[:n_refs], refs[n_refs:]
    tgt, refs = refs[0], refs[1:]
    if last:
        start_ref, refs = refs[0], refs[1:]
    out_refs, refs = refs[: SIDE if last else 1], refs[SIDE if last else 1 :]
    src, acc, sel, k0, k1, s0, s1 = refs
    dims = tgt.shape[1] - TILE
    width = tgt.shape[2]
    targets = tgt.shape[0]
    top = LOCAL * dims
    rows_of_block = src.shape[1]
    vectors = acc.shape[1]
    kb, sb = (k0, k1), (s0, s1)

    for b, (operand, at) in enumerate(places):
        src[b] = source_refs[operand][at : at + rows_of_block]
    row = lax.broadcasted_iota(jnp.int32, (TILE, width), 0)
    for i in range(LOCAL):
        on = (row >= 3 * i) & (row < 3 * i + 3)
        sel[i] = jnp.where(on, jnp.float32(-0.5), jnp.float32(0.0)).astype(jnp.bfloat16)
    if last:
        acc[:targets] = start_ref[...]
    else:
        acc[:targets] = jnp.zeros((targets,) + acc.shape[1:], jnp.float32)
    acc[targets] = jnp.zeros(acc.shape[1:], jnp.float32)
    k1[...] = jnp.zeros_like(k1)

    def picked(p):
        key = keys_ref[p]
        return (key >> 2) & 63, key & 3, (key >> 8) & 255, key >> 16

    def left(b, i, lo, hi):
        at = pl.multiple_of(i * dims, dims)
        return jnp.concatenate(
            [src[b, pl.ds(at, dims), lo:hi], src[b, top : top + TILE, lo:hi]], axis=0
        )

    def right(i, t):
        return jnp.concatenate([tgt[t, :dims], tgt[t, dims:] + sel[i]], axis=0)

    def ahead(p, buffer):
        b, i, t, _ = picked(p)
        rows = right(i, t)
        for lo in range(0, PRE, CHUNK):
            buffer[lo : lo + CHUNK] = tn(left(b, i, lo, lo + CHUNK), rows)

    def gauss(e):
        return jnp.exp2(e * LOG2E).astype(jnp.bfloat16)

    def step(p, k_in, k_out, s_now, s_next):
        b, i, t, _ = picked(p)
        rows = right(i, t)
        for lo in range(0, PRE, CHUNK):
            k_out[lo : lo + CHUNK] = gauss(s_now[lo : lo + CHUNK])
        for lo in range(PRE, width, CHUNK):
            k_out[lo : lo + CHUNK] = gauss(tn(left(b, i, lo, lo + CHUNK), rows))
        ahead(p + 1, s_next)
        b, i, _, a = picked(jnp.maximum(p - 1, 0))
        at = pl.multiple_of(top + TILE + i * vectors, vectors)
        acc[a] += nn(src[b, pl.ds(at, vectors)], k_in[...])

    ahead(0, s0)

    def body(h, carry):
        for u in range(UNROLL):
            step(
                UNROLL * h + u,
                kb[(u + 1) % 2],
                kb[u % 2],
                sb[u % 2],
                sb[(u + 1) % 2],
            )
        return carry

    lax.fori_loop(0, (count_ref[which] + UNROLL) // UNROLL, body, 0)
    if last:
        for d, ref in enumerate(out_refs):
            ref[...] = acc[d * LOCAL : (d + 1) * LOCAL].astype(ref.dtype)
    else:
        out_refs[0][...] = acc[:targets]


SMEM = pl.BlockSpec(memory_space=pltpu.SMEM)
VMEM = pl.BlockSpec(memory_space=pltpu.VMEM)


def pair_sums(which, count, keys, operands, places, tgt, vectors, start=None):
    targets, deep, width = tgt.shape
    dims = deep - TILE
    rows = LOCAL * (dims + vectors) + TILE
    last = start is not None
    if last:
        part = (LOCAL, vectors, width)
        out = [jax.ShapeDtypeStruct(part, jnp.float32)]
        out += [jax.ShapeDtypeStruct(part, jnp.bfloat16)] * (SIDE - 1)
    else:
        out = [jax.ShapeDtypeStruct((targets, vectors, width), jnp.float32)]
    pairs = 40
    return pl.pallas_call(
        functools.partial(pair_kernel, which, places, last),
        out_shape=out,
        in_specs=[SMEM, SMEM] + [VMEM] * (len(operands) + 1 + last),
        out_specs=[VMEM] * len(out),
        scratch_shapes=[
            pltpu.VMEM((len(places), rows, width), jnp.bfloat16),
            pltpu.VMEM((targets + 1, vectors, width), jnp.float32),
            pltpu.VMEM((LOCAL, TILE, width), jnp.bfloat16),
            pltpu.VMEM((width, width), jnp.bfloat16),
            pltpu.VMEM((width, width), jnp.bfloat16),
            pltpu.VMEM((PRE, width), jnp.float32),
            pltpu.VMEM((PRE, width), jnp.float32),
        ],
        compiler_params=pltpu.CompilerParams(vmem_limit_bytes=28 << 20),
        cost_estimate=pl.CostEstimate(
            flops=2 * pairs * width * width * deep,
            transcendentals=pairs * width * width,
            bytes_accessed=len(places) * rows * width * 2,
        ),
        name="pairs_far" if last else "pairs_own",
    )(count, keys, *operands, tgt, *((start,) if last else ()))


def potentials(points, weights, neighbours, counts):
    local, dims, width = points.shape
    vectors = weights.shape[1]
    slots = neighbours.shape[1]
    owners = lax.axis_size("owner")
    helper = lax.axis_index("helper")
    first_leaf = (lax.axis_index("owner") - 1) * GROUP
    up = [(i, (i + 1) % owners) for i in range(owners)]
    down = [(j, i) for i, j in up]

    rows = local * (dims + vectors) + TILE
    source, target = pl.pallas_call(
        pack_kernel,
        out_shape=(
            jax.ShapeDtypeStruct((rows, width), jnp.bfloat16),
            jax.ShapeDtypeStruct((local * dims + TILE, width), jnp.bfloat16),
        ),
        in_specs=[SMEM] + [VMEM] * 4,
        out_specs=(VMEM, VMEM),
        scratch_shapes=[pltpu.VMEM((TILE, width), jnp.float32)],
        compiler_params=pltpu.CompilerParams(vmem_limit_bytes=4 << 20),
        name="pack",
    )(first_leaf[None], points, weights, neighbours, counts[:, None])

    order = (1, 3, 2)
    row = {0: target}
    for d in order:
        row[d] = moved(target, d, 1)
    column = {0: source}
    for d in order:
        column[d] = moved(source, d, 0)
    sides = []
    for ring in (up, down):
        sides.append([lax.ppermute(source, "owner", ring)])
    near = jnp.concatenate([column[1], column[3]], axis=0)
    for ring, side in zip((up, down), sides):
        side.append(lax.ppermute(near, "owner", ring))

    room = SIDE * local * slots + 8
    me = jnp.stack([helper // SIDE, helper % SIDE]).astype(jnp.int32)
    tgt, own, far, count = pl.pallas_call(
        functools.partial(target_kernel, slots),
        out_shape=(
            jax.ShapeDtypeStruct((SIDE * local, dims + TILE, width), jnp.bfloat16),
            jax.ShapeDtypeStruct((room,), jnp.int32),
            jax.ShapeDtypeStruct((room,), jnp.int32),
            jax.ShapeDtypeStruct((2,), jnp.int32),
        ),
        in_specs=[SMEM] + [VMEM] * SIDE,
        out_specs=(VMEM, SMEM, SMEM, SMEM),
        scratch_shapes=[
            pltpu.VMEM((TILE, width), jnp.float32),
            pltpu.VMEM((TILE, width), jnp.float32),
            pltpu.VMEM((SIDE * local, 128), jnp.int32),
            pltpu.SMEM((SIDE * local, 128), jnp.int32),
            pltpu.SemaphoreType.DMA,
        ],
        compiler_params=pltpu.CompilerParams(vmem_limit_bytes=8 << 20),
        name="targets",
    )(me, *[row[d] for d in range(SIDE)])
    opposite, tgt, own, far, count = lax.optimization_barrier(
        (column[2], tgt, own, far, count)
    )
    for ring, side in zip((up, down), sides):
        side.append(lax.ppermute(opposite, "owner", ring))

    (total,) = pair_sums(
        0,
        count,
        own,
        [source, column[1], opposite, column[3]],
        tuple((d, 0) for d in range(SIDE)),
        tgt,
        vectors,
    )
    places = []
    for s in range(2):
        places += [(3 * s, 0), (3 * s + 1, 0), (3 * s + 2, 0), (3 * s + 1, rows)]
    parts = pair_sums(
        1, count, far, sides[0] + sides[1], tuple(places), tgt, vectors, total
    )
    result = parts[0]
    for d in order:
        result = result + moved(parts[d], -d, 1).astype(jnp.float32)
    return result


def solution(mesh):
    placed = (
        P(("owner", "helper"), None, None),
        P(("owner", "helper"), None, None),
        P(("owner", "helper"), None),
        P(("owner", "helper")),
    )
    return jax.shard_map(
        potentials,
        mesh=mesh,
        in_specs=placed,
        out_specs=P(("owner", "helper"), None, None),
        check_vma=False,
    )
```

```python
import functools

import jax
import jax.numpy as jnp
from jax import lax
from jax.experimental import pallas as pl
from jax.experimental.pallas import tpu as pltpu
from jax.sharding import PartitionSpec as P


LOG2E = 1.4426950408889634
SIDE = 4
LOCAL = 4
GROUP = LOCAL * SIDE * SIDE
UNROLL = 8
TAIL = 2
CHUNK = 128
PRE = 128
AT_ONCE = 4
TILE = 16
LISTS = 12
UNUSED = 255


def moved(value, step, along):
    pairs = []
    for h in range(SIDE * SIDE):
        r, c = divmod(h, SIDE)
        if along == 0:
            to = ((r + step) % SIDE) * SIDE + c
        else:
            to = r * SIDE + (c + step) % SIDE
        pairs.append((h, to))
    return lax.ppermute(value, "helper", pairs)


def nn(a, b):
    return lax.dot_general(
        a, b, (((1,), (0,)), ((), ())), preferred_element_type=jnp.float32
    )


def tn(a, b):
    return lax.dot_general(
        a, b, (((0,), (0,)), ((), ())), preferred_element_type=jnp.float32
    )


def pack_kernel(first_ref, counts, points, weights, lists, s_out, t_out, tile, near, sems):
    dims = points.shape[1]
    vectors = weights.shape[1]
    slots = lists.shape[1]
    top = LOCAL * dims
    copies = []
    for i in range(LOCAL):
        here = s_out.at[i * dims : (i + 1) * dims]
        copies.append(pltpu.make_async_copy(points.at[i], here, sems.at[i]))
    for i in range(LOCAL):
        at = top + TILE + i * vectors
        here = s_out.at[at : at + vectors]
        copies.append(pltpu.make_async_copy(weights.at[i], here, sems.at[LOCAL + i]))
    copies.append(pltpu.make_async_copy(lists, near, sems.at[2 * LOCAL]))
    for copy in copies:
        copy.start()
    for i in range(LOCAL):
        copies[i].wait()
        coords = s_out[i * dims : (i + 1) * dims]
        t_out[i * dims : (i + 1) * dims] = coords
        wide = coords.astype(jnp.float32)
        n = jnp.sum(wide * wide, axis=0, keepdims=True)
        high = n.astype(jnp.bfloat16).astype(jnp.float32)
        rest = n - high
        middle = rest.astype(jnp.bfloat16).astype(jnp.float32)
        tile[3 * i : 3 * i + 1] = high
        tile[3 * i + 1 : 3 * i + 2] = middle
        tile[3 * i + 2 : 3 * i + 3] = rest - middle
    tile[LISTS : LISTS + 3] = jnp.ones((3, tile.shape[1]), jnp.float32)
    tile[LISTS + 3 :] = jnp.zeros((1, tile.shape[1]), jnp.float32)
    s_out[top : top + TILE] = tile[...].astype(jnp.bfloat16)
    tile[LISTS:] = jnp.zeros((LOCAL, tile.shape[1]), jnp.float32)
    copies[2 * LOCAL].wait()
    slot = lax.broadcasted_iota(jnp.int32, (1, slots), 1)
    for i in range(LOCAL):
        size = counts[i]
        place = jnp.where(slot < size, near[i : i + 1] - first_ref[0], UNUSED)
        tile[LISTS + i : LISTS + i + 1, :slots] = place.astype(jnp.float32)
        tile[LISTS + i : LISTS + i + 1, slots : slots + 1] = jnp.full(
            (1, 1), size, jnp.int32
        ).astype(jnp.float32)
    t_out[top:] = tile[...].astype(jnp.bfloat16)
    for copy in copies[LOCAL : 2 * LOCAL]:
        copy.wait()


def target_kernel(slots, me_ref, *refs):
    blocks, refs = refs[:SIDE], refs[SIDE:]
    tgt, own_ref, far_ref, count_ref, tile, norm, keys, keys_s, sem = refs
    dims = tgt.shape[1] - TILE
    top = LOCAL * dims
    norm[...] = jnp.full(norm.shape, -0.5, jnp.float32)
    norm[LISTS + 3 :] = jnp.zeros((1, norm.shape[1]), jnp.float32)
    for b, ref in enumerate(blocks):
        tile[...] = ref[top:].astype(jnp.float32)
        keys[b * LOCAL : (b + 1) * LOCAL] = tile[LISTS:, :128].astype(jnp.int32)
    s = keys[...]
    g, h, i = s >> 6, (s >> 2) & 15, s & 3
    used = s < UNUSED
    lane = lax.broadcasted_iota(jnp.int32, s.shape, 1)
    t = lax.broadcasted_iota(jnp.int32, s.shape, 0)
    block = ((me_ref[0] - (h >> 2)) & 3) * LOCAL + i
    slot = jnp.where(used, block + jnp.where(g == 2, SIDE * LOCAL, 0), 0)
    mine = used & ((h & 3) == me_ref[1])
    kind = jnp.where(mine, jnp.where(g == 1, 0, 1), 2)
    key = (kind << 24) | (t << 16) | (t << 8) | slot
    keys[...] = jnp.where(lane == slots, s, key)
    copy = pltpu.make_async_copy(keys, keys_s, sem)
    copy.start()
    for b, ref in enumerate(blocks):
        tile[...] = ref[top:].astype(jnp.float32)
        for j in range(LOCAL):
            tgt[b * LOCAL + j, :dims] = ref[j * dims : (j + 1) * dims]
            norm[LISTS : LISTS + 3] = -0.5 * tile[3 * j : 3 * j + 3]
            tgt[b * LOCAL + j, dims:] = norm[...].astype(jnp.bfloat16)
    copy.wait()

    def per_target(t, carry):
        def some(q, carry):
            own, far = carry
            for u in range(AT_ONCE):
                key = keys_s[t, AT_ONCE * q + u]
                kind = key >> 24
                own_ref[own] = key & 0xFFFFFF
                far_ref[far] = key & 0xFFFFFF
                own = own + jnp.where(kind == 0, 1, 0)
                far = far + jnp.where(kind == 1, 1, 0)
            return own, far

        turns = (keys_s[t, slots] + (AT_ONCE - 1)) >> 2
        return lax.fori_loop(0, turns, some, carry)

    targets = SIDE * LOCAL
    own, far = lax.fori_loop(0, targets, per_target, (jnp.int32(0), jnp.int32(0)))
    count_ref[0] = own
    count_ref[1] = far
    for u in range(UNROLL + 2):
        own_ref[own + u] = jnp.int32(targets << 16)
        far_ref[far + u] = jnp.int32(targets << 16)


def pair_kernel(which, places, last, count_ref, keys_ref, *refs):
    n_refs = 1 + max(p[0] for p in places)
    source_refs, refs = refs[:n_refs], refs[n_refs:]
    tgt, refs = refs[0], refs[1:]
    if last:
        start_ref, refs = refs[0], refs[1:]
    out_refs, refs = refs[: SIDE if last else 1], refs[SIDE if last else 1 :]
    src, wts, acc, k0, k1, s0, s1 = refs
    dims = tgt.shape[1] - TILE
    width = tgt.shape[2]
    targets = tgt.shape[0]
    top = LOCAL * dims
    vectors = acc.shape[1]
    kb, sb = (k0, k1), (s0, s1)

    row = lax.broadcasted_iota(jnp.int32, (TILE, width), 0)
    for b, (operand, at) in enumerate(places):
        block = source_refs[operand]
        tile = block[at + top : at + top + TILE].astype(jnp.float32)
        for i in range(LOCAL):
            on = ((row >= 3 * i) & (row < 3 * i + 3)) | (row >= LISTS)
            slot = b * LOCAL + i
            src[slot, :dims] = block[at + i * dims : at + (i + 1) * dims]
            src[slot, dims:] = jnp.where(on, tile, 0.0).astype(jnp.bfloat16)
            first = at + top + TILE + i * vectors
            wts[slot] = block[first : first + vectors]
    if last:
        acc[:targets] = start_ref[...]
    else:
        acc[:targets] = jnp.zeros((targets,) + acc.shape[1:], jnp.float32)
    acc[targets] = jnp.zeros(acc.shape[1:], jnp.float32)
    k1[...] = jnp.zeros_like(k1)

    def picked(p):
        key = keys_ref[p]
        return key & 255, (key >> 8) & 255, key >> 16

    def ahead(p, buffer):
        s, t, _ = picked(p)
        rows = tgt[t]
        for lo in range(0, PRE, CHUNK):
            buffer[lo : lo + CHUNK] = tn(src[s, :, lo : lo + CHUNK], rows)

    def gauss(e):
        return jnp.exp2(e * LOG2E).astype(jnp.bfloat16)

    def step(p, k_in, k_out, s_now, s_next):
        s, t, _ = picked(p)
        rows = tgt[t]
        for lo in range(0, PRE, CHUNK):
            k_out[lo : lo + CHUNK] = gauss(s_now[lo : lo + CHUNK])
        for lo in range(PRE, width, CHUNK):
            k_out[lo : lo + CHUNK] = gauss(tn(src[s, :, lo : lo + CHUNK], rows))
        ahead(p + 1, s_next)
        s, _, a = picked(jnp.maximum(p - 1, 0))
        acc[a] += nn(wts[s], k_in[...])

    ahead(0, s0)

    def turn(first, steps):
        for u in range(steps):
            step(
                first + u,
                kb[(u + 1) % 2],
                kb[u % 2],
                sb[u % 2],
                sb[(u + 1) % 2],
            )

    def body(h, carry):
        turn(UNROLL * h, UNROLL)
        return carry

    def tail(h, carry):
        turn(whole + TAIL * h, TAIL)
        return carry

    steps = count_ref[which] + 1
    turns = steps // UNROLL
    whole = turns * UNROLL
    lax.fori_loop(0, turns, body, 0)
    lax.fori_loop(0, (steps - whole + TAIL - 1) // TAIL, tail, 0)
    if last:
        for d, ref in enumerate(out_refs):
            ref[...] = acc[d * LOCAL : (d + 1) * LOCAL].astype(ref.dtype)
    else:
        out_refs[0][...] = acc[:targets]


SMEM = pl.BlockSpec(memory_space=pltpu.SMEM)
VMEM = pl.BlockSpec(memory_space=pltpu.VMEM)
HBM = pl.BlockSpec(memory_space=pltpu.HBM)


def pair_sums(which, count, keys, operands, places, tgt, vectors, start=None):
    targets, deep, width = tgt.shape
    dims = deep - TILE
    rows = LOCAL * (dims + vectors) + TILE
    last = start is not None
    if last:
        part = (LOCAL, vectors, width)
        out = [jax.ShapeDtypeStruct(part, jnp.float32)]
        out += [jax.ShapeDtypeStruct(part, jnp.bfloat16)] * (SIDE - 1)
    else:
        out = [jax.ShapeDtypeStruct((targets, vectors, width), jnp.float32)]
    pairs = 40
    return pl.pallas_call(
        functools.partial(pair_kernel, which, places, last),
        out_shape=out,
        in_specs=[SMEM, SMEM] + [VMEM] * (len(operands) + 1 + last),
        out_specs=[VMEM] * len(out),
        scratch_shapes=[
            pltpu.VMEM((len(places) * LOCAL, deep, width), jnp.bfloat16),
            pltpu.VMEM((len(places) * LOCAL, vectors, width), jnp.bfloat16),
            pltpu.VMEM((targets + 1, vectors, width), jnp.float32),
            pltpu.VMEM((width, width), jnp.bfloat16),
            pltpu.VMEM((width, width), jnp.bfloat16),
            pltpu.VMEM((PRE, width), jnp.float32),
            pltpu.VMEM((PRE, width), jnp.float32),
        ],
        compiler_params=pltpu.CompilerParams(vmem_limit_bytes=28 << 20),
        cost_estimate=pl.CostEstimate(
            flops=2 * pairs * width * width * deep,
            transcendentals=pairs * width * width,
            bytes_accessed=len(places) * rows * width * 2,
        ),
        name="pairs_far" if last else "pairs_own",
    )(count, keys, *operands, tgt, *((start,) if last else ()))


def potentials(points, weights, neighbours, counts):
    local, dims, width = points.shape
    vectors = weights.shape[1]
    slots = neighbours.shape[1]
    owners = lax.axis_size("owner")
    helper = lax.axis_index("helper")
    first_leaf = (lax.axis_index("owner") - 1) * GROUP
    up = [(i, (i + 1) % owners) for i in range(owners)]
    down = [(j, i) for i, j in up]

    rows = local * (dims + vectors) + TILE
    source, target = pl.pallas_call(
        pack_kernel,
        out_shape=(
            jax.ShapeDtypeStruct((rows, width), jnp.bfloat16),
            jax.ShapeDtypeStruct((local * dims + TILE, width), jnp.bfloat16),
        ),
        in_specs=[SMEM, SMEM] + [HBM] * 3,
        out_specs=(VMEM, VMEM),
        scratch_shapes=[
            pltpu.VMEM((TILE, width), jnp.float32),
            pltpu.VMEM((local, slots), jnp.int32),
            pltpu.SemaphoreType.DMA((2 * local + 1,)),
        ],
        compiler_params=pltpu.CompilerParams(vmem_limit_bytes=4 << 20),
        name="pack",
    )(
        first_leaf[None],
        counts,
        *[
            pltpu.with_memory_space_constraint(a, pltpu.HBM)
            for a in (points, weights, neighbours)
        ],
    )

    order = (1, 3, 2)
    row = {0: target}
    for d in order:
        row[d] = moved(target, d, 1)
    column = {0: source}
    for d in order:
        column[d] = moved(source, d, 0)
    sides = []
    for ring in (up, down):
        sides.append([lax.ppermute(source, "owner", ring)])
    for d in order[:2]:
        for ring, side in zip((up, down), sides):
            side.append(lax.ppermute(column[d], "owner", ring))

    room = SIDE * local * slots + 8
    me = jnp.stack([helper // SIDE, helper % SIDE]).astype(jnp.int32)
    make_targets = pl.pallas_call(
        functools.partial(target_kernel, slots),
        out_shape=(
            jax.ShapeDtypeStruct((SIDE * local, dims + TILE, width), jnp.bfloat16),
            jax.ShapeDtypeStruct((room,), jnp.int32),
            jax.ShapeDtypeStruct((room,), jnp.int32),
            jax.ShapeDtypeStruct((2,), jnp.int32),
        ),
        in_specs=[SMEM] + [VMEM] * SIDE,
        out_specs=(VMEM, SMEM, SMEM, SMEM),
        scratch_shapes=[
            pltpu.VMEM((TILE, width), jnp.float32),
            pltpu.VMEM((TILE, width), jnp.float32),
            pltpu.VMEM((SIDE * local, 128), jnp.int32),
            pltpu.SMEM((SIDE * local, 128), jnp.int32),
            pltpu.SemaphoreType.DMA,
        ],
        compiler_params=pltpu.CompilerParams(vmem_limit_bytes=8 << 20),
        name="targets",
    )
    tgt, own, far, count = make_targets(me, *[row[d] for d in range(SIDE)])
    opposite, tgt, own, far, count = lax.optimization_barrier(
        (column[2], tgt, own, far, count)
    )
    for ring, side in zip((up, down), sides):
        side.append(lax.ppermute(opposite, "owner", ring))

    (total,) = pair_sums(
        0,
        count,
        own,
        [source, column[1], opposite, column[3]],
        tuple((d, 0) for d in range(SIDE)),
        tgt,
        vectors,
    )
    places = []
    for s in range(2):
        places += [(4 * s, 0), (4 * s + 1, 0), (4 * s + 3, 0), (4 * s + 2, 0)]
    parts = pair_sums(
        1, count, far, sides[0] + sides[1], tuple(places), tgt, vectors, total
    )
    result = parts[0]
    for d in order:
        result = result + moved(parts[d], -d, 1).astype(jnp.float32)
    return result


def solution(mesh):
    placed = (
        P(("owner", "helper"), None, None),
        P(("owner", "helper"), None, None),
        P(("owner", "helper"), None),
        P(("owner", "helper")),
    )
    return jax.shard_map(
        potentials,
        mesh=mesh,
        in_specs=placed,
        out_specs=P(("owner", "helper"), None, None),
        check_vma=False,
    )
```

```python
import functools

import jax
import jax.numpy as jnp
from jax import lax
from jax.experimental import pallas as pl
from jax.experimental.pallas import tpu as pltpu
from jax.sharding import PartitionSpec as P


LOG2E = 1.4426950408889634
SIDE = 4
LOCAL = 4
GROUP = LOCAL * SIDE * SIDE
UNROLL = 8
TAIL = 2
CHUNK = 128
PRE = 128
AT_ONCE = 4
TILE = 16
LISTS = 12
UNUSED = 255


def moved(value, step, along):
    pairs = []
    for h in range(SIDE * SIDE):
        r, c = divmod(h, SIDE)
        if along == 0:
            to = ((r + step) % SIDE) * SIDE + c
        else:
            to = r * SIDE + (c + step) % SIDE
        pairs.append((h, to))
    return lax.ppermute(value, "helper", pairs)


def nn(a, b):
    return lax.dot_general(
        a, b, (((1,), (0,)), ((), ())), preferred_element_type=jnp.float32
    )


def tn(a, b):
    return lax.dot_general(
        a, b, (((0,), (0,)), ((), ())), preferred_element_type=jnp.float32
    )


def pack_kernel(
    first_ref, counts_hbm, points, weights, lists, s_out, t_out, tile, near, counts, sems
):
    dims = points.shape[1]
    vectors = weights.shape[1]
    slots = lists.shape[1]
    top = LOCAL * dims
    copies = []
    for i in range(LOCAL):
        here = s_out.at[i * dims : (i + 1) * dims]
        copies.append(pltpu.make_async_copy(points.at[i], here, sems.at[i]))
    for i in range(LOCAL):
        at = top + TILE + i * vectors
        here = s_out.at[at : at + vectors]
        copies.append(pltpu.make_async_copy(weights.at[i], here, sems.at[LOCAL + i]))
    copies.append(pltpu.make_async_copy(lists, near, sems.at[2 * LOCAL]))
    copies.append(pltpu.make_async_copy(counts_hbm, counts, sems.at[2 * LOCAL + 1]))
    for copy in copies:
        copy.start()
    for i in range(LOCAL):
        copies[i].wait()
        coords = s_out[i * dims : (i + 1) * dims]
        t_out[i * dims : (i + 1) * dims] = coords
        wide = coords.astype(jnp.float32)
        n = jnp.sum(wide * wide, axis=0, keepdims=True)
        high = n.astype(jnp.bfloat16).astype(jnp.float32)
        rest = n - high
        middle = rest.astype(jnp.bfloat16).astype(jnp.float32)
        tile[3 * i : 3 * i + 1] = high
        tile[3 * i + 1 : 3 * i + 2] = middle
        tile[3 * i + 2 : 3 * i + 3] = rest - middle
    tile[LISTS : LISTS + 3] = jnp.ones((3, tile.shape[1]), jnp.float32)
    tile[LISTS + 3 :] = jnp.zeros((1, tile.shape[1]), jnp.float32)
    s_out[top : top + TILE] = tile[...].astype(jnp.bfloat16)
    tile[LISTS:] = jnp.zeros((LOCAL, tile.shape[1]), jnp.float32)
    copies[2 * LOCAL].wait()
    copies[2 * LOCAL + 1].wait()
    slot = lax.broadcasted_iota(jnp.int32, (1, slots), 1)
    for i in range(LOCAL):
        size = counts[i]
        place = jnp.where(slot < size, near[i : i + 1] - first_ref[0], UNUSED)
        tile[LISTS + i : LISTS + i + 1, :slots] = place.astype(jnp.float32)
        tile[LISTS + i : LISTS + i + 1, slots : slots + 1] = jnp.full(
            (1, 1), size, jnp.int32
        ).astype(jnp.float32)
    t_out[top:] = tile[...].astype(jnp.bfloat16)
    for copy in copies[LOCAL : 2 * LOCAL]:
        copy.wait()


def join_kernel(a, b, c, out):
    rows = a.shape[0]
    for i, ref in enumerate((a, b, c)):
        out[i * rows : (i + 1) * rows] = ref[...]


def target_kernel(slots, me_ref, *refs):
    blocks, refs = refs[:SIDE], refs[SIDE:]
    tgt, own_ref, far_ref, tile, norm, keys, keys_s, sem = refs
    dims = tgt.shape[1] - TILE
    top = LOCAL * dims
    norm[...] = jnp.full(norm.shape, -0.5, jnp.float32)
    norm[LISTS + 3 :] = jnp.zeros((1, norm.shape[1]), jnp.float32)
    for b, ref in enumerate(blocks):
        tile[...] = ref[top:].astype(jnp.float32)
        keys[b * LOCAL : (b + 1) * LOCAL] = tile[LISTS:, :128].astype(jnp.int32)
    s = keys[...]
    g, h, i = s >> 6, (s >> 2) & 15, s & 3
    used = s < UNUSED
    lane = lax.broadcasted_iota(jnp.int32, s.shape, 1)
    t = lax.broadcasted_iota(jnp.int32, s.shape, 0)
    block = ((me_ref[0] - (h >> 2)) & 3) * LOCAL + i
    slot = jnp.where(used, block + jnp.where(g == 2, SIDE * LOCAL, 0), 0)
    mine = used & ((h & 3) == me_ref[1])
    kind = jnp.where(mine, jnp.where(g == 1, 0, 1), 2)
    key = (kind << 24) | (t << 16) | (t << 8) | slot
    keys[...] = jnp.where(lane == slots, s, key)
    copy = pltpu.make_async_copy(keys, keys_s, sem)
    copy.start()
    for b, ref in enumerate(blocks):
        tile[...] = ref[top:].astype(jnp.float32)
        for j in range(LOCAL):
            tgt[b * LOCAL + j, :dims] = ref[j * dims : (j + 1) * dims]
            norm[LISTS : LISTS + 3] = -0.5 * tile[3 * j : 3 * j + 3]
            tgt[b * LOCAL + j, dims:] = norm[...].astype(jnp.bfloat16)
    copy.wait()

    def per_target(t, carry):
        def some(q, carry):
            own, far = carry
            for u in range(AT_ONCE):
                key = keys_s[t, AT_ONCE * q + u]
                kind = key >> 24
                own_ref[own + 1] = key & 0xFFFFFF
                far_ref[far + 1] = key & 0xFFFFFF
                own = own + jnp.where(kind == 0, 1, 0)
                far = far + jnp.where(kind == 1, 1, 0)
            return own, far

        turns = (keys_s[t, slots] + (AT_ONCE - 1)) >> 2
        return lax.fori_loop(0, turns, some, carry)

    targets = SIDE * LOCAL
    own, far = lax.fori_loop(0, targets, per_target, (jnp.int32(0), jnp.int32(0)))
    own_ref[0] = own
    far_ref[0] = far
    for u in range(1, TAIL + 3):
        own_ref[own + u] = jnp.int32(targets << 16)
        far_ref[far + u] = jnp.int32(targets << 16)


def pair_kernel(places, last, keys_ref, *refs):
    n_refs = 1 + max(p[0] for p in places)
    source_refs, refs = refs[:n_refs], refs[n_refs:]
    tgt, refs = refs[0], refs[1:]
    if last:
        start_ref, refs = refs[0], refs[1:]
    out_refs, refs = refs[: SIDE if last else 1], refs[SIDE if last else 1 :]
    src, wts, acc, k0, k1, s0, s1 = refs
    dims = tgt.shape[1] - TILE
    width = tgt.shape[2]
    targets = tgt.shape[0]
    top = LOCAL * dims
    vectors = acc.shape[1]
    kb, sb = (k0, k1), (s0, s1)

    row = lax.broadcasted_iota(jnp.int32, (TILE, width), 0)
    for b, (operand, at) in enumerate(places):
        block = source_refs[operand]
        tile = block[at + top : at + top + TILE].astype(jnp.float32)
        for i in range(LOCAL):
            on = ((row >= 3 * i) & (row < 3 * i + 3)) | (row >= LISTS)
            slot = b * LOCAL + i
            src[slot, :dims] = block[at + i * dims : at + (i + 1) * dims]
            src[slot, dims:] = jnp.where(on, tile, 0.0).astype(jnp.bfloat16)
            first = at + top + TILE + i * vectors
            wts[slot] = block[first : first + vectors]
    if last:
        acc[:targets] = start_ref[...]
    else:
        acc[:targets] = jnp.zeros((targets,) + acc.shape[1:], jnp.float32)
    acc[targets] = jnp.zeros(acc.shape[1:], jnp.float32)
    k1[...] = jnp.zeros_like(k1)

    def picked(p):
        key = keys_ref[p + 1]
        return key & 255, (key >> 8) & 255, key >> 16

    def ahead(p, buffer):
        s, t, _ = picked(p)
        rows = tgt[t]
        for lo in range(0, PRE, CHUNK):
            buffer[lo : lo + CHUNK] = tn(src[s, :, lo : lo + CHUNK], rows)

    def gauss(e):
        return jnp.exp2(e * LOG2E).astype(jnp.bfloat16)

    def step(p, k_in, k_out, s_now, s_next):
        s, t, _ = picked(p)
        rows = tgt[t]
        for lo in range(0, PRE, CHUNK):
            k_out[lo : lo + CHUNK] = gauss(s_now[lo : lo + CHUNK])
        for lo in range(PRE, width, CHUNK):
            k_out[lo : lo + CHUNK] = gauss(tn(src[s, :, lo : lo + CHUNK], rows))
        ahead(p + 1, s_next)
        s, _, a = picked(jnp.maximum(p - 1, 0))
        acc[a] += nn(wts[s], k_in[...])

    ahead(0, s0)

    def turn(first, steps):
        for u in range(steps):
            step(
                first + u,
                kb[(u + 1) % 2],
                kb[u % 2],
                sb[u % 2],
                sb[(u + 1) % 2],
            )

    def body(h, carry):
        turn(UNROLL * h, UNROLL)
        return carry

    def tail(h, carry):
        turn(whole + TAIL * h, TAIL)
        return carry

    steps = keys_ref[0] + 1
    turns = steps // UNROLL
    whole = turns * UNROLL
    lax.fori_loop(0, turns, body, 0)
    lax.fori_loop(0, (steps - whole + TAIL - 1) // TAIL, tail, 0)
    if last:
        for d, ref in enumerate(out_refs):
            ref[...] = acc[d * LOCAL : (d + 1) * LOCAL].astype(ref.dtype)
    else:
        out_refs[0][...] = acc[:targets]


SMEM = pl.BlockSpec(memory_space=pltpu.SMEM)
VMEM = pl.BlockSpec(memory_space=pltpu.VMEM)
HBM = pl.BlockSpec(memory_space=pltpu.HBM)


def pair_sums(keys, operands, places, tgt, vectors, start=None):
    targets, deep, width = tgt.shape
    dims = deep - TILE
    rows = LOCAL * (dims + vectors) + TILE
    last = start is not None
    if last:
        part = (LOCAL, vectors, width)
        out = [jax.ShapeDtypeStruct(part, jnp.float32)]
        out += [jax.ShapeDtypeStruct(part, jnp.bfloat16)] * (SIDE - 1)
    else:
        out = [jax.ShapeDtypeStruct((targets, vectors, width), jnp.float32)]
    pairs = 40
    return pl.pallas_call(
        functools.partial(pair_kernel, places, last),
        out_shape=out,
        in_specs=[SMEM] + [VMEM] * (len(operands) + 1 + last),
        out_specs=[VMEM] * len(out),
        scratch_shapes=[
            pltpu.VMEM((len(places) * LOCAL, deep, width), jnp.bfloat16),
            pltpu.VMEM((len(places) * LOCAL, vectors, width), jnp.bfloat16),
            pltpu.VMEM((targets + 1, vectors, width), jnp.float32),
            pltpu.VMEM((width, width), jnp.bfloat16),
            pltpu.VMEM((width, width), jnp.bfloat16),
            pltpu.VMEM((PRE, width), jnp.float32),
            pltpu.VMEM((PRE, width), jnp.float32),
        ],
        compiler_params=pltpu.CompilerParams(vmem_limit_bytes=14 << 20),
        cost_estimate=pl.CostEstimate(
            flops=2 * pairs * width * width * deep,
            transcendentals=pairs * width * width,
            bytes_accessed=len(places) * rows * width * 2,
        ),
        name="pairs_far" if last else "pairs_own",
    )(keys, *operands, tgt, *((start,) if last else ()))


def potentials(points, weights, neighbours, counts):
    local, dims, width = points.shape
    vectors = weights.shape[1]
    slots = neighbours.shape[1]
    owners = lax.axis_size("owner")
    helper = lax.axis_index("helper")
    first_leaf = (lax.axis_index("owner") - 1) * GROUP
    up = [(i, (i + 1) % owners) for i in range(owners)]
    down = [(j, i) for i, j in up]

    rows = local * (dims + vectors) + TILE
    source, target = pl.pallas_call(
        pack_kernel,
        out_shape=(
            jax.ShapeDtypeStruct((rows, width), jnp.bfloat16),
            jax.ShapeDtypeStruct((local * dims + TILE, width), jnp.bfloat16),
        ),
        in_specs=[SMEM] + [HBM] * 4,
        out_specs=(VMEM, VMEM),
        scratch_shapes=[
            pltpu.VMEM((TILE, width), jnp.float32),
            pltpu.VMEM((local, slots), jnp.int32),
            pltpu.SMEM((local,), jnp.int32),
            pltpu.SemaphoreType.DMA((2 * local + 2,)),
        ],
        compiler_params=pltpu.CompilerParams(vmem_limit_bytes=4 << 20),
        name="pack",
    )(
        first_leaf[None],
        *[
            pltpu.with_memory_space_constraint(a, pltpu.HBM)
            for a in (counts, points, weights, neighbours)
        ],
    )

    order = (1, 3, 2)
    row = {0: target}
    for d in order:
        row[d] = moved(target, d, 1)
    column = {0: source}
    for d in order:
        column[d] = moved(source, d, 0)
    join = pl.pallas_call(
        join_kernel,
        out_shape=jax.ShapeDtypeStruct((3 * rows, width), jnp.bfloat16),
        in_specs=[VMEM] * 3,
        out_specs=VMEM,
        compiler_params=pltpu.CompilerParams(vmem_limit_bytes=4 << 20),
        name="join",
    )
    near = join(source, column[1], column[3])
    sides = []
    for ring in (up, down):
        sides.append([lax.ppermute(near, "owner", ring)])

    room = SIDE * local * slots + 8
    me = jnp.stack([helper // SIDE, helper % SIDE]).astype(jnp.int32)
    make_targets = pl.pallas_call(
        functools.partial(target_kernel, slots),
        out_shape=(
            jax.ShapeDtypeStruct((SIDE * local, dims + TILE, width), jnp.bfloat16),
            jax.ShapeDtypeStruct((room,), jnp.int32),
            jax.ShapeDtypeStruct((room,), jnp.int32),
        ),
        in_specs=[SMEM] + [VMEM] * SIDE,
        out_specs=(VMEM, SMEM, SMEM),
        scratch_shapes=[
            pltpu.VMEM((TILE, width), jnp.float32),
            pltpu.VMEM((TILE, width), jnp.float32),
            pltpu.VMEM((SIDE * local, 128), jnp.int32),
            pltpu.SMEM((SIDE * local, 128), jnp.int32),
            pltpu.SemaphoreType.DMA,
        ],
        compiler_params=pltpu.CompilerParams(vmem_limit_bytes=8 << 20),
        name="targets",
    )
    tgt, own, far = make_targets(me, *[row[d] for d in range(SIDE)])
    opposite, tgt, own, far = lax.optimization_barrier((column[2], tgt, own, far))
    for ring, side in zip((up, down), sides):
        side.append(lax.ppermute(opposite, "owner", ring))

    (total,) = pair_sums(
        own,
        [source, column[1], opposite, column[3]],
        tuple((d, 0) for d in range(SIDE)),
        tgt,
        vectors,
    )
    places = []
    for s in range(2):
        places += [(2 * s, 0), (2 * s, rows), (2 * s + 1, 0), (2 * s, 2 * rows)]
    parts = pair_sums(far, sides[0] + sides[1], tuple(places), tgt, vectors, total)
    result = parts[0]
    for d in order:
        result = result + moved(parts[d], -d, 1).astype(jnp.float32)
    return result


def solution(mesh):
    placed = (
        P(("owner", "helper"), None, None),
        P(("owner", "helper"), None, None),
        P(("owner", "helper"), None),
        P(("owner", "helper")),
    )
    return jax.shard_map(
        potentials,
        mesh=mesh,
        in_specs=placed,
        out_specs=P(("owner", "helper"), None, None),
        check_vma=False,
    )
```

```python
import functools

import jax
import jax.numpy as jnp
from jax import lax
from jax.experimental import pallas as pl
from jax.experimental.pallas import tpu as pltpu
from jax.sharding import PartitionSpec as P


LOG2E = 1.4426950408889634
SIDE = 4
LOCAL = 4
GROUP = LOCAL * SIDE * SIDE
UNROLL = 8
TAIL = 2
CHUNK = 128
PRE = 128
AT_ONCE = 4
TILE = 16
LISTS = 12
UNUSED = 255


def moved(value, step, along):
    pairs = []
    for h in range(SIDE * SIDE):
        r, c = divmod(h, SIDE)
        if along == 0:
            to = ((r + step) % SIDE) * SIDE + c
        else:
            to = r * SIDE + (c + step) % SIDE
        pairs.append((h, to))
    return lax.ppermute(value, "helper", pairs)


def nn(a, b):
    return lax.dot_general(
        a, b, (((1,), (0,)), ((), ())), preferred_element_type=jnp.float32
    )


def tn(a, b):
    return lax.dot_general(
        a, b, (((0,), (0,)), ((), ())), preferred_element_type=jnp.float32
    )


def pack_kernel(
    first_ref, counts_hbm, points, weights, lists, s_out, t_out, tile, near, counts, sems
):
    dims = points.shape[1]
    vectors = weights.shape[1]
    slots = lists.shape[1]
    top = LOCAL * dims
    copies = []
    for i in range(LOCAL):
        here = s_out.at[i * dims : (i + 1) * dims]
        copies.append(pltpu.make_async_copy(points.at[i], here, sems.at[i]))
    for i in range(LOCAL):
        at = top + TILE + i * vectors
        here = s_out.at[at : at + vectors]
        copies.append(pltpu.make_async_copy(weights.at[i], here, sems.at[LOCAL + i]))
    copies.append(pltpu.make_async_copy(lists, near, sems.at[2 * LOCAL]))
    copies.append(pltpu.make_async_copy(counts_hbm, counts, sems.at[2 * LOCAL + 1]))
    for copy in copies:
        copy.start()
    for i in range(LOCAL):
        copies[i].wait()
        coords = s_out[i * dims : (i + 1) * dims]
        t_out[i * dims : (i + 1) * dims] = coords
        wide = coords.astype(jnp.float32)
        n = jnp.sum(wide * wide, axis=0, keepdims=True)
        high = n.astype(jnp.bfloat16).astype(jnp.float32)
        rest = n - high
        middle = rest.astype(jnp.bfloat16).astype(jnp.float32)
        tile[3 * i : 3 * i + 1] = high
        tile[3 * i + 1 : 3 * i + 2] = middle
        tile[3 * i + 2 : 3 * i + 3] = rest - middle
    tile[LISTS : LISTS + 3] = jnp.ones((3, tile.shape[1]), jnp.float32)
    tile[LISTS + 3 :] = jnp.zeros((1, tile.shape[1]), jnp.float32)
    s_out[top : top + TILE] = tile[...].astype(jnp.bfloat16)
    tile[LISTS:] = jnp.zeros((LOCAL, tile.shape[1]), jnp.float32)
    copies[2 * LOCAL].wait()
    copies[2 * LOCAL + 1].wait()
    slot = lax.broadcasted_iota(jnp.int32, (1, slots), 1)
    for i in range(LOCAL):
        size = counts[i]
        place = jnp.where(slot < size, near[i : i + 1] - first_ref[0], UNUSED)
        tile[LISTS + i : LISTS + i + 1, :slots] = place.astype(jnp.float32)
        tile[LISTS + i : LISTS + i + 1, slots : slots + 1] = jnp.full(
            (1, 1), size, jnp.int32
        ).astype(jnp.float32)
    t_out[top:] = tile[...].astype(jnp.bfloat16)
    for copy in copies[LOCAL : 2 * LOCAL]:
        copy.wait()


def join_kernel(a, b, out):
    rows = a.shape[0]
    out[:rows] = a[...]
    out[rows:] = b[...]


def target_kernel(slots, me_ref, *refs):
    blocks, refs = refs[:SIDE], refs[SIDE:]
    tgt, own_ref, far_ref, tile, norm, keys, keys_s, sem = refs
    dims = tgt.shape[1] - TILE
    top = LOCAL * dims
    norm[...] = jnp.full(norm.shape, -0.5, jnp.float32)
    norm[LISTS + 3 :] = jnp.zeros((1, norm.shape[1]), jnp.float32)
    for b, ref in enumerate(blocks):
        tile[...] = ref[top:].astype(jnp.float32)
        keys[b * LOCAL : (b + 1) * LOCAL] = tile[LISTS:, :128].astype(jnp.int32)
    s = keys[...]
    g, h, i = s >> 6, (s >> 2) & 15, s & 3
    used = s < UNUSED
    lane = lax.broadcasted_iota(jnp.int32, s.shape, 1)
    t = lax.broadcasted_iota(jnp.int32, s.shape, 0)
    block = ((me_ref[0] - (h >> 2)) & 3) * LOCAL + i
    slot = jnp.where(used, block + jnp.where(g == 2, SIDE * LOCAL, 0), 0)
    mine = used & ((h & 3) == me_ref[1])
    kind = jnp.where(mine, jnp.where(g == 1, 0, 1), 2)
    key = (kind << 24) | (t << 16) | (t << 8) | slot
    keys[...] = jnp.where(lane == slots, s, key)
    copy = pltpu.make_async_copy(keys, keys_s, sem)
    copy.start()
    for b, ref in enumerate(blocks):
        tile[...] = ref[top:].astype(jnp.float32)
        for j in range(LOCAL):
            tgt[b * LOCAL + j, :dims] = ref[j * dims : (j + 1) * dims]
            norm[LISTS : LISTS + 3] = -0.5 * tile[3 * j : 3 * j + 3]
            tgt[b * LOCAL + j, dims:] = norm[...].astype(jnp.bfloat16)
    copy.wait()

    def per_target(t, carry):
        def some(q, carry):
            own, far = carry
            for u in range(AT_ONCE):
                key = keys_s[t, AT_ONCE * q + u]
                kind = key >> 24
                own_ref[own + 1] = key & 0xFFFFFF
                far_ref[far + 1] = key & 0xFFFFFF
                own = own + jnp.where(kind == 0, 1, 0)
                far = far + jnp.where(kind == 1, 1, 0)
            return own, far

        turns = (keys_s[t, slots] + (AT_ONCE - 1)) >> 2
        return lax.fori_loop(0, turns, some, carry)

    targets = SIDE * LOCAL
    own, far = lax.fori_loop(0, targets, per_target, (jnp.int32(0), jnp.int32(0)))
    own_ref[0] = own
    far_ref[0] = far
    for u in range(1, TAIL + 3):
        own_ref[own + u] = jnp.int32(targets << 16)
        far_ref[far + u] = jnp.int32(targets << 16)


def pair_kernel(places, last, keys_ref, *refs):
    n_refs = 1 + max(p[0] for p in places)
    source_refs, refs = refs[:n_refs], refs[n_refs:]
    tgt, refs = refs[0], refs[1:]
    if last:
        start_ref, refs = refs[0], refs[1:]
    out_refs, refs = refs[: SIDE if last else 1], refs[SIDE if last else 1 :]
    src, wts, acc, k0, k1, s0, s1 = refs
    dims = tgt.shape[1] - TILE
    width = tgt.shape[2]
    targets = tgt.shape[0]
    top = LOCAL * dims
    vectors = acc.shape[1]
    kb, sb = (k0, k1), (s0, s1)

    row = lax.broadcasted_iota(jnp.int32, (TILE, width), 0)
    for b, (operand, at) in enumerate(places):
        block = source_refs[operand]
        tile = block[at + top : at + top + TILE].astype(jnp.float32)
        for i in range(LOCAL):
            on = ((row >= 3 * i) & (row < 3 * i + 3)) | (row >= LISTS)
            slot = b * LOCAL + i
            src[slot, :dims] = block[at + i * dims : at + (i + 1) * dims]
            src[slot, dims:] = jnp.where(on, tile, 0.0).astype(jnp.bfloat16)
            first = at + top + TILE + i * vectors
            wts[slot] = block[first : first + vectors]
    if last:
        acc[:targets] = start_ref[...]
    else:
        acc[:targets] = jnp.zeros((targets,) + acc.shape[1:], jnp.float32)
    acc[targets] = jnp.zeros(acc.shape[1:], jnp.float32)
    k1[...] = jnp.zeros_like(k1)

    def picked(p):
        key = keys_ref[p + 1]
        return key & 255, (key >> 8) & 255, key >> 16

    def ahead(p, buffer):
        s, t, _ = picked(p)
        rows = tgt[t]
        for lo in range(0, PRE, CHUNK):
            buffer[lo : lo + CHUNK] = tn(src[s, :, lo : lo + CHUNK], rows)

    def gauss(e):
        return jnp.exp2(e * LOG2E).astype(jnp.bfloat16)

    def step(p, k_in, k_out, s_now, s_next):
        s, t, _ = picked(p)
        rows = tgt[t]
        for lo in range(0, PRE, CHUNK):
            k_out[lo : lo + CHUNK] = gauss(s_now[lo : lo + CHUNK])
        for lo in range(PRE, width, CHUNK):
            k_out[lo : lo + CHUNK] = gauss(tn(src[s, :, lo : lo + CHUNK], rows))
        ahead(p + 1, s_next)
        s, _, a = picked(jnp.maximum(p - 1, 0))
        acc[a] += nn(wts[s], k_in[...])

    ahead(0, s0)

    def turn(first, steps):
        for u in range(steps):
            step(
                first + u,
                kb[(u + 1) % 2],
                kb[u % 2],
                sb[u % 2],
                sb[(u + 1) % 2],
            )

    def body(h, carry):
        turn(UNROLL * h, UNROLL)
        return carry

    def tail(h, carry):
        turn(whole + TAIL * h, TAIL)
        return carry

    steps = keys_ref[0] + 1
    turns = steps // UNROLL
    whole = turns * UNROLL
    lax.fori_loop(0, turns, body, 0)
    lax.fori_loop(0, (steps - whole + TAIL - 1) // TAIL, tail, 0)
    if last:
        for d, ref in enumerate(out_refs):
            ref[...] = acc[d * LOCAL : (d + 1) * LOCAL].astype(ref.dtype)
    else:
        out_refs[0][...] = acc[:targets]


SMEM = pl.BlockSpec(memory_space=pltpu.SMEM)
VMEM = pl.BlockSpec(memory_space=pltpu.VMEM)
HBM = pl.BlockSpec(memory_space=pltpu.HBM)


def pair_sums(keys, operands, places, tgt, vectors, start=None):
    targets, deep, width = tgt.shape
    dims = deep - TILE
    rows = LOCAL * (dims + vectors) + TILE
    last = start is not None
    if last:
        part = (LOCAL, vectors, width)
        out = [jax.ShapeDtypeStruct(part, jnp.float32)]
        out += [jax.ShapeDtypeStruct(part, jnp.bfloat16)] * (SIDE - 1)
    else:
        out = [jax.ShapeDtypeStruct((targets, vectors, width), jnp.float32)]
    pairs = 40
    return pl.pallas_call(
        functools.partial(pair_kernel, places, last),
        out_shape=out,
        in_specs=[SMEM] + [VMEM] * (len(operands) + 1 + last),
        out_specs=[VMEM] * len(out),
        scratch_shapes=[
            pltpu.VMEM((len(places) * LOCAL, deep, width), jnp.bfloat16),
            pltpu.VMEM((len(places) * LOCAL, vectors, width), jnp.bfloat16),
            pltpu.VMEM((targets + 1, vectors, width), jnp.float32),
            pltpu.VMEM((width, width), jnp.bfloat16),
            pltpu.VMEM((width, width), jnp.bfloat16),
            pltpu.VMEM((PRE, width), jnp.float32),
            pltpu.VMEM((PRE, width), jnp.float32),
        ],
        compiler_params=pltpu.CompilerParams(vmem_limit_bytes=14 << 20),
        cost_estimate=pl.CostEstimate(
            flops=2 * pairs * width * width * deep,
            transcendentals=pairs * width * width,
            bytes_accessed=len(places) * rows * width * 2,
        ),
        name="pairs_far" if last else "pairs_own",
    )(keys, *operands, tgt, *((start,) if last else ()))


def potentials(points, weights, neighbours, counts):
    local, dims, width = points.shape
    vectors = weights.shape[1]
    slots = neighbours.shape[1]
    owners = lax.axis_size("owner")
    helper = lax.axis_index("helper")
    first_leaf = (lax.axis_index("owner") - 1) * GROUP
    up = [(i, (i + 1) % owners) for i in range(owners)]
    down = [(j, i) for i, j in up]

    rows = local * (dims + vectors) + TILE
    source, target = pl.pallas_call(
        pack_kernel,
        out_shape=(
            jax.ShapeDtypeStruct((rows, width), jnp.bfloat16),
            jax.ShapeDtypeStruct((local * dims + TILE, width), jnp.bfloat16),
        ),
        in_specs=[SMEM] + [HBM] * 4,
        out_specs=(VMEM, VMEM),
        scratch_shapes=[
            pltpu.VMEM((TILE, width), jnp.float32),
            pltpu.VMEM((local, slots), jnp.int32),
            pltpu.SMEM((local,), jnp.int32),
            pltpu.SemaphoreType.DMA((2 * local + 2,)),
        ],
        compiler_params=pltpu.CompilerParams(vmem_limit_bytes=4 << 20),
        name="pack",
    )(
        first_leaf[None],
        *[
            pltpu.with_memory_space_constraint(a, pltpu.HBM)
            for a in (counts, points, weights, neighbours)
        ],
    )

    order = (1, 3, 2)
    row = {0: target}
    for d in order:
        row[d] = moved(target, d, 1)
    column = {0: source}
    for d in order:
        column[d] = moved(source, d, 0)
    join = pl.pallas_call(
        join_kernel,
        out_shape=jax.ShapeDtypeStruct((2 * rows, width), jnp.bfloat16),
        in_specs=[VMEM] * 2,
        out_specs=VMEM,
        compiler_params=pltpu.CompilerParams(vmem_limit_bytes=4 << 20),
        name="join",
    )
    sides = []
    for ring in (up, down):
        sides.append([lax.ppermute(source, "owner", ring)])
    near = join(column[1], column[3])
    for ring, side in zip((up, down), sides):
        side.append(lax.ppermute(near, "owner", ring))

    room = SIDE * local * slots + 8
    me = jnp.stack([helper // SIDE, helper % SIDE]).astype(jnp.int32)
    make_targets = pl.pallas_call(
        functools.partial(target_kernel, slots),
        out_shape=(
            jax.ShapeDtypeStruct((SIDE * local, dims + TILE, width), jnp.bfloat16),
            jax.ShapeDtypeStruct((room,), jnp.int32),
            jax.ShapeDtypeStruct((room,), jnp.int32),
        ),
        in_specs=[SMEM] + [VMEM] * SIDE,
        out_specs=(VMEM, SMEM, SMEM),
        scratch_shapes=[
            pltpu.VMEM((TILE, width), jnp.float32),
            pltpu.VMEM((TILE, width), jnp.float32),
            pltpu.VMEM((SIDE * local, 128), jnp.int32),
            pltpu.SMEM((SIDE * local, 128), jnp.int32),
            pltpu.SemaphoreType.DMA,
        ],
        compiler_params=pltpu.CompilerParams(vmem_limit_bytes=8 << 20),
        name="targets",
    )
    tgt, own, far = make_targets(me, *[row[d] for d in range(SIDE)])
    opposite, tgt, own, far = lax.optimization_barrier((column[2], tgt, own, far))
    for ring, side in zip((up, down), sides):
        side.append(lax.ppermute(opposite, "owner", ring))

    (total,) = pair_sums(
        own,
        [source, column[1], opposite, column[3]],
        tuple((d, 0) for d in range(SIDE)),
        tgt,
        vectors,
    )
    places = []
    for s in range(2):
        places += [(3 * s, 0), (3 * s + 1, 0), (3 * s + 2, 0), (3 * s + 1, rows)]
    parts = pair_sums(far, sides[0] + sides[1], tuple(places), tgt, vectors, total)
    result = parts[0]
    for d in order:
        result = result + moved(parts[d], -d, 1).astype(jnp.float32)
    return result


def solution(mesh):
    placed = (
        P(("owner", "helper"), None, None),
        P(("owner", "helper"), None, None),
        P(("owner", "helper"), None),
        P(("owner", "helper")),
    )
    return jax.shard_map(
        potentials,
        mesh=mesh,
        in_specs=placed,
        out_specs=P(("owner", "helper"), None, None),
        check_vma=False,
    )
```

```python
import functools

import jax
import jax.numpy as jnp
from jax import lax
from jax.experimental import pallas as pl
from jax.experimental.pallas import tpu as pltpu
from jax.sharding import PartitionSpec as P


LOG2E = 1.4426950408889634
SIDE = 4
LOCAL = 4
GROUP = LOCAL * SIDE * SIDE
UNROLL = 8
TAIL = 2
CHUNK = 128
PRE = 128
AT_ONCE = 4
TILE = 16
LISTS = 12
UNUSED = 255


def moved(value, step, along):
    pairs = []
    for h in range(SIDE * SIDE):
        r, c = divmod(h, SIDE)
        if along == 0:
            to = ((r + step) % SIDE) * SIDE + c
        else:
            to = r * SIDE + (c + step) % SIDE
        pairs.append((h, to))
    return lax.ppermute(value, "helper", pairs)


def nn(a, b):
    return lax.dot_general(
        a, b, (((1,), (0,)), ((), ())), preferred_element_type=jnp.float32
    )


def tn(a, b):
    return lax.dot_general(
        a, b, (((0,), (0,)), ((), ())), preferred_element_type=jnp.float32
    )


def pack_kernel(
    first_ref, counts_hbm, points, weights, lists, s_out, t_out, tile, near, counts, sems
):
    dims = points.shape[1]
    vectors = weights.shape[1]
    slots = lists.shape[1]
    top = LOCAL * dims
    copies = []
    for i in range(LOCAL):
        here = s_out.at[i * dims : (i + 1) * dims]
        copies.append(pltpu.make_async_copy(points.at[i], here, sems.at[i]))
    for i in range(LOCAL):
        at = top + TILE + i * vectors
        here = s_out.at[at : at + vectors]
        copies.append(pltpu.make_async_copy(weights.at[i], here, sems.at[LOCAL + i]))
    copies.append(pltpu.make_async_copy(lists, near, sems.at[2 * LOCAL]))
    copies.append(pltpu.make_async_copy(counts_hbm, counts, sems.at[2 * LOCAL + 1]))
    for copy in copies:
        copy.start()
    for i in range(LOCAL):
        copies[i].wait()
        coords = s_out[i * dims : (i + 1) * dims]
        t_out[i * dims : (i + 1) * dims] = coords
        wide = coords.astype(jnp.float32)
        n = jnp.sum(wide * wide, axis=0, keepdims=True)
        high = n.astype(jnp.bfloat16).astype(jnp.float32)
        rest = n - high
        middle = rest.astype(jnp.bfloat16).astype(jnp.float32)
        tile[3 * i : 3 * i + 1] = high
        tile[3 * i + 1 : 3 * i + 2] = middle
        tile[3 * i + 2 : 3 * i + 3] = rest - middle
    tile[LISTS : LISTS + 3] = jnp.ones((3, tile.shape[1]), jnp.float32)
    tile[LISTS + 3 :] = jnp.zeros((1, tile.shape[1]), jnp.float32)
    s_out[top : top + TILE] = tile[...].astype(jnp.bfloat16)
    tile[LISTS:] = jnp.zeros((LOCAL, tile.shape[1]), jnp.float32)
    copies[2 * LOCAL].wait()
    copies[2 * LOCAL + 1].wait()
    slot = lax.broadcasted_iota(jnp.int32, (1, slots), 1)
    for i in range(LOCAL):
        size = counts[i]
        place = jnp.where(slot < size, near[i : i + 1] - first_ref[0], UNUSED)
        tile[LISTS + i : LISTS + i + 1, :slots] = place.astype(jnp.float32)
        tile[LISTS + i : LISTS + i + 1, slots : slots + 1] = jnp.full(
            (1, 1), size, jnp.int32
        ).astype(jnp.float32)
    t_out[top:] = tile[...].astype(jnp.bfloat16)
    for copy in copies[LOCAL : 2 * LOCAL]:
        copy.wait()


def join_kernel(a, b, out):
    rows = a.shape[0]
    out[:rows] = a[...]
    out[rows:] = b[...]


def target_kernel(slots, me_ref, *refs):
    blocks, refs = refs[:SIDE], refs[SIDE:]
    tgt, own_ref, far_ref, tile, norm, keys, keys_s, sem = refs
    dims = tgt.shape[1] - TILE
    top = LOCAL * dims
    norm[...] = jnp.full(norm.shape, -0.5, jnp.float32)
    norm[LISTS + 3 :] = jnp.zeros((1, norm.shape[1]), jnp.float32)
    for b, ref in enumerate(blocks):
        tile[...] = ref[top:].astype(jnp.float32)
        keys[b * LOCAL : (b + 1) * LOCAL] = tile[LISTS:, :128].astype(jnp.int32)
    s = keys[...]
    g, h, i = s >> 6, (s >> 2) & 15, s & 3
    used = s < UNUSED
    lane = lax.broadcasted_iota(jnp.int32, s.shape, 1)
    t = lax.broadcasted_iota(jnp.int32, s.shape, 0)
    block = ((me_ref[0] - (h >> 2)) & 3) * LOCAL + i
    slot = jnp.where(used, block + jnp.where(g == 2, SIDE * LOCAL, 0), 0)
    mine = used & ((h & 3) == me_ref[1])
    kind = jnp.where(mine, jnp.where(g == 1, 0, 1), 2)
    key = (kind << 24) | (t << 16) | (t << 8) | slot
    keys[...] = jnp.where(lane == slots, s, key)
    copy = pltpu.make_async_copy(keys, keys_s, sem)
    copy.start()
    for b, ref in enumerate(blocks):
        tile[...] = ref[top:].astype(jnp.float32)
        for j in range(LOCAL):
            tgt[b * LOCAL + j, :dims] = ref[j * dims : (j + 1) * dims]
            norm[LISTS : LISTS + 3] = -0.5 * tile[3 * j : 3 * j + 3]
            tgt[b * LOCAL + j, dims:] = norm[...].astype(jnp.bfloat16)
    copy.wait()

    def per_target(t, carry):
        def some(q, carry):
            own, far = carry
            for u in range(AT_ONCE):
                key = keys_s[t, AT_ONCE * q + u]
                kind = key >> 24
                own_ref[own + 1] = key & 0xFFFFFF
                far_ref[far + 1] = key & 0xFFFFFF
                own = own + jnp.where(kind == 0, 1, 0)
                far = far + jnp.where(kind == 1, 1, 0)
            return own, far

        turns = (keys_s[t, slots] + (AT_ONCE - 1)) >> 2
        return lax.fori_loop(0, turns, some, carry)

    targets = SIDE * LOCAL
    own, far = lax.fori_loop(0, targets, per_target, (jnp.int32(0), jnp.int32(0)))
    own_ref[0] = own
    far_ref[0] = far
    for u in range(1, TAIL + 3):
        own_ref[own + u] = jnp.int32(targets << 16)
        far_ref[far + u] = jnp.int32(targets << 16)


def pair_kernel(places, last, keys_ref, *refs):
    n_refs = 1 + max(p[0] for p in places)
    source_refs, refs = refs[:n_refs], refs[n_refs:]
    tgt, refs = refs[0], refs[1:]
    if last:
        start_ref, refs = refs[0], refs[1:]
    out_refs, refs = refs[: SIDE if last else 1], refs[SIDE if last else 1 :]
    src, wts, acc, k0, k1, s0, s1 = refs
    dims = tgt.shape[1] - TILE
    width = tgt.shape[2]
    targets = tgt.shape[0]
    top = LOCAL * dims
    vectors = acc.shape[1]
    kb, sb = (k0, k1), (s0, s1)

    row = lax.broadcasted_iota(jnp.int32, (TILE, width), 0)
    for b, (operand, at) in enumerate(places):
        block = source_refs[operand]
        tile = block[at + top : at + top + TILE].astype(jnp.float32)
        for i in range(LOCAL):
            on = ((row >= 3 * i) & (row < 3 * i + 3)) | (row >= LISTS)
            slot = b * LOCAL + i
            src[slot, :dims] = block[at + i * dims : at + (i + 1) * dims]
            src[slot, dims:] = jnp.where(on, tile, 0.0).astype(jnp.bfloat16)
            first = at + top + TILE + i * vectors
            wts[slot] = block[first : first + vectors]
    if last:
        acc[:targets] = start_ref[...]
    else:
        acc[:targets] = jnp.zeros((targets,) + acc.shape[1:], jnp.float32)
    acc[targets] = jnp.zeros(acc.shape[1:], jnp.float32)
    k1[...] = jnp.zeros_like(k1)

    def picked(p):
        key = keys_ref[p + 1]
        return key & 255, (key >> 8) & 255, key >> 16

    def ahead(p, buffer):
        s, t, _ = picked(p)
        rows = tgt[t]
        for lo in range(0, PRE, CHUNK):
            buffer[lo : lo + CHUNK] = tn(src[s, :, lo : lo + CHUNK], rows)

    def gauss(e):
        return jnp.exp2(e * LOG2E).astype(jnp.bfloat16)

    def step(p, k_in, k_out, s_now, s_next):
        s, t, _ = picked(p)
        rows = tgt[t]
        for lo in range(0, PRE, CHUNK):
            k_out[lo : lo + CHUNK] = gauss(s_now[lo : lo + CHUNK])
        for lo in range(PRE, width, CHUNK):
            k_out[lo : lo + CHUNK] = gauss(tn(src[s, :, lo : lo + CHUNK], rows))
        ahead(p + 1, s_next)
        s, _, a = picked(jnp.maximum(p - 1, 0))
        acc[a] += nn(wts[s], k_in[...])

    ahead(0, s0)

    def turn(first, steps):
        for u in range(steps):
            step(
                first + u,
                kb[(u + 1) % 2],
                kb[u % 2],
                sb[u % 2],
                sb[(u + 1) % 2],
            )

    def body(h, carry):
        turn(UNROLL * h, UNROLL)
        return carry

    def tail(h, carry):
        turn(whole + TAIL * h, TAIL)
        return carry

    steps = keys_ref[0] + 1
    turns = steps // UNROLL
    whole = turns * UNROLL
    lax.fori_loop(0, turns, body, 0)
    lax.fori_loop(0, (steps - whole + TAIL - 1) // TAIL, tail, 0)
    if last:
        for d, ref in enumerate(out_refs):
            ref[...] = acc[d * LOCAL : (d + 1) * LOCAL].astype(ref.dtype)
    else:
        out_refs[0][...] = acc[:targets]


SMEM = pl.BlockSpec(memory_space=pltpu.SMEM)
VMEM = pl.BlockSpec(memory_space=pltpu.VMEM)
HBM = pl.BlockSpec(memory_space=pltpu.HBM)


def pair_sums(keys, operands, places, tgt, vectors, start=None):
    targets, deep, width = tgt.shape
    dims = deep - TILE
    rows = LOCAL * (dims + vectors) + TILE
    last = start is not None
    if last:
        part = (LOCAL, vectors, width)
        out = [jax.ShapeDtypeStruct(part, jnp.float32)]
        out += [jax.ShapeDtypeStruct(part, jnp.bfloat16)] * (SIDE - 1)
    else:
        out = [jax.ShapeDtypeStruct((targets, vectors, width), jnp.float32)]
    pairs = 40
    return pl.pallas_call(
        functools.partial(pair_kernel, places, last),
        out_shape=out,
        in_specs=[SMEM] + [VMEM] * (len(operands) + 1 + last),
        out_specs=[VMEM] * len(out),
        scratch_shapes=[
            pltpu.VMEM((len(places) * LOCAL, deep, width), jnp.bfloat16),
            pltpu.VMEM((len(places) * LOCAL, vectors, width), jnp.bfloat16),
            pltpu.VMEM((targets + 1, vectors, width), jnp.float32),
            pltpu.VMEM((width, width), jnp.bfloat16),
            pltpu.VMEM((width, width), jnp.bfloat16),
            pltpu.VMEM((PRE, width), jnp.float32),
            pltpu.VMEM((PRE, width), jnp.float32),
        ],
        compiler_params=pltpu.CompilerParams(vmem_limit_bytes=14 << 20),
        cost_estimate=pl.CostEstimate(
            flops=2 * pairs * width * width * deep,
            transcendentals=pairs * width * width,
            bytes_accessed=len(places) * rows * width * 2,
        ),
        name="pairs_far" if last else "pairs_own",
    )(keys, *operands, tgt, *((start,) if last else ()))


def potentials(points, weights, neighbours, counts):
    local, dims, width = points.shape
    vectors = weights.shape[1]
    slots = neighbours.shape[1]
    owners = lax.axis_size("owner")
    helper = lax.axis_index("helper")
    first_leaf = (lax.axis_index("owner") - 1) * GROUP
    up = [(i, (i + 1) % owners) for i in range(owners)]
    down = [(j, i) for i, j in up]

    rows = local * (dims + vectors) + TILE
    source, target = pl.pallas_call(
        pack_kernel,
        out_shape=(
            jax.ShapeDtypeStruct((rows, width), jnp.bfloat16),
            jax.ShapeDtypeStruct((local * dims + TILE, width), jnp.bfloat16),
        ),
        in_specs=[SMEM] + [HBM] * 4,
        out_specs=(VMEM, VMEM),
        scratch_shapes=[
            pltpu.VMEM((TILE, width), jnp.float32),
            pltpu.VMEM((local, slots), jnp.int32),
            pltpu.SMEM((local,), jnp.int32),
            pltpu.SemaphoreType.DMA((2 * local + 2,)),
        ],
        compiler_params=pltpu.CompilerParams(vmem_limit_bytes=4 << 20),
        name="pack",
    )(
        first_leaf[None],
        *[
            pltpu.with_memory_space_constraint(a, pltpu.HBM)
            for a in (counts, points, weights, neighbours)
        ],
    )

    order = (1, 3, 2)
    row = {0: target}
    for d in order:
        row[d] = moved(target, d, 1)
    column = {0: source}
    for d in order:
        column[d] = moved(source, d, 0)
    join = pl.pallas_call(
        join_kernel,
        out_shape=jax.ShapeDtypeStruct((2 * rows, width), jnp.bfloat16),
        in_specs=[VMEM] * 2,
        out_specs=VMEM,
        compiler_params=pltpu.CompilerParams(vmem_limit_bytes=4 << 20),
        name="join",
    )
    sides = []
    for ring in (up, down):
        sides.append([lax.ppermute(source, "owner", ring)])
    for d in order[:2]:
        for ring, side in zip((up, down), sides):
            side.append(lax.ppermute(column[d], "owner", ring))

    room = SIDE * local * slots + 8
    me = jnp.stack([helper // SIDE, helper % SIDE]).astype(jnp.int32)
    make_targets = pl.pallas_call(
        functools.partial(target_kernel, slots),
        out_shape=(
            jax.ShapeDtypeStruct((SIDE * local, dims + TILE, width), jnp.bfloat16),
            jax.ShapeDtypeStruct((room,), jnp.int32),
            jax.ShapeDtypeStruct((room,), jnp.int32),
        ),
        in_specs=[SMEM] + [VMEM] * SIDE,
        out_specs=(VMEM, SMEM, SMEM),
        scratch_shapes=[
            pltpu.VMEM((TILE, width), jnp.float32),
            pltpu.VMEM((TILE, width), jnp.float32),
            pltpu.VMEM((SIDE * local, 128), jnp.int32),
            pltpu.SMEM((SIDE * local, 128), jnp.int32),
            pltpu.SemaphoreType.DMA,
        ],
        compiler_params=pltpu.CompilerParams(vmem_limit_bytes=8 << 20),
        name="targets",
    )
    tgt, own, far = make_targets(me, *[row[d] for d in range(SIDE)])
    opposite, tgt, own, far = lax.optimization_barrier((column[2], tgt, own, far))
    for ring, side in zip((up, down), sides):
        side.append(lax.ppermute(opposite, "owner", ring))

    (total,) = pair_sums(
        own,
        [source, column[1], opposite, column[3]],
        tuple((d, 0) for d in range(SIDE)),
        tgt,
        vectors,
    )
    places = []
    for s in range(2):
        places += [(4 * s, 0), (4 * s + 1, 0), (4 * s + 3, 0), (4 * s + 2, 0)]
    parts = pair_sums(far, sides[0] + sides[1], tuple(places), tgt, vectors, total)
    result = parts[0]
    for d in order:
        result = result + moved(parts[d], -d, 1).astype(jnp.float32)
    return result


def solution(mesh):
    placed = (
        P(("owner", "helper"), None, None),
        P(("owner", "helper"), None, None),
        P(("owner", "helper"), None),
        P(("owner", "helper")),
    )
    return jax.shard_map(
        potentials,
        mesh=mesh,
        in_specs=placed,
        out_specs=P(("owner", "helper"), None, None),
        check_vma=False,
    )
```

```python
import functools

import jax
import jax.numpy as jnp
from jax import lax
from jax.experimental import pallas as pl
from jax.experimental.pallas import tpu as pltpu
from jax.sharding import PartitionSpec as P


LOG2E = 1.4426950408889634
SIDE = 4
LOCAL = 4
GROUP = LOCAL * SIDE * SIDE
UNROLL = 8
TAIL = 2
CHUNK = 128
PRE = 128
AT_ONCE = 4
TILE = 16
LISTS = 12
UNUSED = 255


def moved(value, step, along):
    pairs = []
    for h in range(SIDE * SIDE):
        r, c = divmod(h, SIDE)
        if along == 0:
            to = ((r + step) % SIDE) * SIDE + c
        else:
            to = r * SIDE + (c + step) % SIDE
        pairs.append((h, to))
    return lax.ppermute(value, "helper", pairs)


def nn(a, b):
    return lax.dot_general(
        a, b, (((1,), (0,)), ((), ())), preferred_element_type=jnp.float32
    )


def tn(a, b):
    return lax.dot_general(
        a, b, (((0,), (0,)), ((), ())), preferred_element_type=jnp.float32
    )


def pack_kernel(
    first_ref,
    counts_hbm,
    points,
    weights,
    lists,
    s_out,
    t_out,
    l_out,
    tile,
    near,
    counts,
    sems,
):
    dims = points.shape[1]
    vectors = weights.shape[1]
    slots = lists.shape[1]
    top = LOCAL * dims
    copies = []
    for i in range(LOCAL):
        here = s_out.at[i * dims : (i + 1) * dims]
        copies.append(pltpu.make_async_copy(points.at[i], here, sems.at[i]))
    for i in range(LOCAL):
        at = top + TILE + i * vectors
        here = s_out.at[at : at + vectors]
        copies.append(pltpu.make_async_copy(weights.at[i], here, sems.at[LOCAL + i]))
    copies.append(pltpu.make_async_copy(lists, near, sems.at[2 * LOCAL]))
    copies.append(pltpu.make_async_copy(counts_hbm, counts, sems.at[2 * LOCAL + 1]))
    for copy in copies:
        copy.start()
    for i in range(LOCAL):
        copies[i].wait()
        coords = s_out[i * dims : (i + 1) * dims]
        t_out[i * dims : (i + 1) * dims] = coords
        wide = coords.astype(jnp.float32)
        n = jnp.sum(wide * wide, axis=0, keepdims=True)
        high = n.astype(jnp.bfloat16).astype(jnp.float32)
        rest = n - high
        middle = rest.astype(jnp.bfloat16).astype(jnp.float32)
        tile[3 * i : 3 * i + 1] = high
        tile[3 * i + 1 : 3 * i + 2] = middle
        tile[3 * i + 2 : 3 * i + 3] = rest - middle
    tile[LISTS : LISTS + 3] = jnp.ones((3, tile.shape[1]), jnp.float32)
    tile[LISTS + 3 :] = jnp.zeros((1, tile.shape[1]), jnp.float32)
    s_out[top : top + TILE] = tile[...].astype(jnp.bfloat16)
    t_out[top:] = tile[...].astype(jnp.bfloat16)
    l_out[...] = jnp.zeros_like(l_out)
    copies[2 * LOCAL].wait()
    copies[2 * LOCAL + 1].wait()
    slot = lax.broadcasted_iota(jnp.int32, (1, slots), 1)
    for i in range(LOCAL):
        size = counts[i]
        place = jnp.where(slot < size, near[i : i + 1] - first_ref[0], UNUSED)
        l_out[i : i + 1, :slots] = place
        l_out[i : i + 1, slots : slots + 1] = jnp.full((1, 1), size, jnp.int32)
    for copy in copies[LOCAL : 2 * LOCAL]:
        copy.wait()


def join_kernel(a, b, out):
    rows = a.shape[0]
    out[:rows] = a[...]
    out[rows:] = b[...]


def list_kernel(slots, me_ref, *refs):
    blocks, refs = refs[:SIDE], refs[SIDE:]
    own_ref, far_ref, keys, keys_s, sem = refs
    for b, ref in enumerate(blocks):
        keys[b * LOCAL : (b + 1) * LOCAL] = ref[...]
    s = keys[...]
    g, h, i = s >> 6, (s >> 2) & 15, s & 3
    used = s < UNUSED
    lane = lax.broadcasted_iota(jnp.int32, s.shape, 1)
    t = lax.broadcasted_iota(jnp.int32, s.shape, 0)
    block = ((me_ref[0] - (h >> 2)) & 3) * LOCAL + i
    slot = jnp.where(used, block + jnp.where(g == 2, SIDE * LOCAL, 0), 0)
    mine = used & ((h & 3) == me_ref[1])
    kind = jnp.where(mine, jnp.where(g == 1, 0, 1), 2)
    key = (kind << 24) | (t << 16) | (t << 8) | slot
    keys[...] = jnp.where(lane == slots, s, key)
    copy = pltpu.make_async_copy(keys, keys_s, sem)
    copy.start()
    copy.wait()

    def per_target(t, carry):
        def some(q, carry):
            own, far = carry
            for u in range(AT_ONCE):
                key = keys_s[t, AT_ONCE * q + u]
                kind = key >> 24
                own_ref[own + 1] = key & 0xFFFFFF
                far_ref[far + 1] = key & 0xFFFFFF
                own = own + jnp.where(kind == 0, 1, 0)
                far = far + jnp.where(kind == 1, 1, 0)
            return own, far

        turns = (keys_s[t, slots] + (AT_ONCE - 1)) >> 2
        return lax.fori_loop(0, turns, some, carry)

    targets = SIDE * LOCAL
    own, far = lax.fori_loop(0, targets, per_target, (jnp.int32(0), jnp.int32(0)))
    own_ref[0] = own
    far_ref[0] = far
    for u in range(1, TAIL + 3):
        own_ref[own + u] = jnp.int32(targets << 16)
        far_ref[far + u] = jnp.int32(targets << 16)


def target_kernel(*refs):
    blocks, (tgt, tile, norm) = refs[:SIDE], refs[SIDE:]
    dims = tgt.shape[1] - TILE
    top = LOCAL * dims
    norm[...] = jnp.full(norm.shape, -0.5, jnp.float32)
    norm[LISTS + 3 :] = jnp.zeros((1, norm.shape[1]), jnp.float32)
    for b, ref in enumerate(blocks):
        tile[...] = ref[top:].astype(jnp.float32)
        for j in range(LOCAL):
            tgt[b * LOCAL + j, :dims] = ref[j * dims : (j + 1) * dims]
            norm[LISTS : LISTS + 3] = -0.5 * tile[3 * j : 3 * j + 3]
            tgt[b * LOCAL + j, dims:] = norm[...].astype(jnp.bfloat16)


def pair_kernel(places, last, keys_ref, *refs):
    n_refs = 1 + max(p[0] for p in places)
    source_refs, refs = refs[:n_refs], refs[n_refs:]
    tgt, refs = refs[0], refs[1:]
    if last:
        start_ref, refs = refs[0], refs[1:]
    out_refs, refs = refs[: SIDE if last else 1], refs[SIDE if last else 1 :]
    src, wts, acc, k0, k1, s0, s1 = refs
    dims = tgt.shape[1] - TILE
    width = tgt.shape[2]
    targets = tgt.shape[0]
    top = LOCAL * dims
    vectors = acc.shape[1]
    kb, sb = (k0, k1), (s0, s1)

    row = lax.broadcasted_iota(jnp.int32, (TILE, width), 0)
    for b, (operand, at) in enumerate(places):
        block = source_refs[operand]
        tile = block[at + top : at + top + TILE].astype(jnp.float32)
        for i in range(LOCAL):
            on = ((row >= 3 * i) & (row < 3 * i + 3)) | (row >= LISTS)
            slot = b * LOCAL + i
            src[slot, :dims] = block[at + i * dims : at + (i + 1) * dims]
            src[slot, dims:] = jnp.where(on, tile, 0.0).astype(jnp.bfloat16)
            first = at + top + TILE + i * vectors
            wts[slot] = block[first : first + vectors]
    if last:
        acc[:targets] = start_ref[...]
    else:
        acc[:targets] = jnp.zeros((targets,) + acc.shape[1:], jnp.float32)
    acc[targets] = jnp.zeros(acc.shape[1:], jnp.float32)
    k1[...] = jnp.zeros_like(k1)

    def picked(p):
        key = keys_ref[p + 1]
        return key & 255, (key >> 8) & 255, key >> 16

    def ahead(p, buffer):
        s, t, _ = picked(p)
        rows = tgt[t]
        for lo in range(0, PRE, CHUNK):
            buffer[lo : lo + CHUNK] = tn(src[s, :, lo : lo + CHUNK], rows)

    def gauss(e):
        return jnp.exp2(e * LOG2E).astype(jnp.bfloat16)

    def step(p, k_in, k_out, s_now, s_next):
        s, t, _ = picked(p)
        rows = tgt[t]
        for lo in range(0, PRE, CHUNK):
            k_out[lo : lo + CHUNK] = gauss(s_now[lo : lo + CHUNK])
        for lo in range(PRE, width, CHUNK):
            k_out[lo : lo + CHUNK] = gauss(tn(src[s, :, lo : lo + CHUNK], rows))
        ahead(p + 1, s_next)
        s, _, a = picked(jnp.maximum(p - 1, 0))
        acc[a] += nn(wts[s], k_in[...])

    ahead(0, s0)

    def turn(first, steps):
        for u in range(steps):
            step(
                first + u,
                kb[(u + 1) % 2],
                kb[u % 2],
                sb[u % 2],
                sb[(u + 1) % 2],
            )

    def body(h, carry):
        turn(UNROLL * h, UNROLL)
        return carry

    def tail(h, carry):
        turn(whole + TAIL * h, TAIL)
        return carry

    steps = keys_ref[0] + 1
    turns = steps // UNROLL
    whole = turns * UNROLL
    lax.fori_loop(0, turns, body, 0)
    lax.fori_loop(0, (steps - whole + TAIL - 1) // TAIL, tail, 0)
    if last:
        for d, ref in enumerate(out_refs):
            ref[...] = acc[d * LOCAL : (d + 1) * LOCAL].astype(ref.dtype)
    else:
        out_refs[0][...] = acc[:targets]


SMEM = pl.BlockSpec(memory_space=pltpu.SMEM)
VMEM = pl.BlockSpec(memory_space=pltpu.VMEM)
HBM = pl.BlockSpec(memory_space=pltpu.HBM)


def pair_sums(keys, operands, places, tgt, vectors, start=None):
    targets, deep, width = tgt.shape
    dims = deep - TILE
    rows = LOCAL * (dims + vectors) + TILE
    last = start is not None
    if last:
        part = (LOCAL, vectors, width)
        out = [jax.ShapeDtypeStruct(part, jnp.float32)]
        out += [jax.ShapeDtypeStruct(part, jnp.bfloat16)] * (SIDE - 1)
    else:
        out = [jax.ShapeDtypeStruct((targets, vectors, width), jnp.float32)]
    pairs = 40
    return pl.pallas_call(
        functools.partial(pair_kernel, places, last),
        out_shape=out,
        in_specs=[SMEM] + [VMEM] * (len(operands) + 1 + last),
        out_specs=[VMEM] * len(out),
        scratch_shapes=[
            pltpu.VMEM((len(places) * LOCAL, deep, width), jnp.bfloat16),
            pltpu.VMEM((len(places) * LOCAL, vectors, width), jnp.bfloat16),
            pltpu.VMEM((targets + 1, vectors, width), jnp.float32),
            pltpu.VMEM((width, width), jnp.bfloat16),
            pltpu.VMEM((width, width), jnp.bfloat16),
            pltpu.VMEM((PRE, width), jnp.float32),
            pltpu.VMEM((PRE, width), jnp.float32),
        ],
        compiler_params=pltpu.CompilerParams(vmem_limit_bytes=14 << 20),
        cost_estimate=pl.CostEstimate(
            flops=2 * pairs * width * width * deep,
            transcendentals=pairs * width * width,
            bytes_accessed=len(places) * rows * width * 2,
        ),
        name="pairs_far" if last else "pairs_own",
    )(keys, *operands, tgt, *((start,) if last else ()))


def potentials(points, weights, neighbours, counts):
    local, dims, width = points.shape
    vectors = weights.shape[1]
    slots = neighbours.shape[1]
    owners = lax.axis_size("owner")
    helper = lax.axis_index("helper")
    first_leaf = (lax.axis_index("owner") - 1) * GROUP
    up = [(i, (i + 1) % owners) for i in range(owners)]
    down = [(j, i) for i, j in up]

    rows = local * (dims + vectors) + TILE
    source, target, listed = pl.pallas_call(
        pack_kernel,
        out_shape=(
            jax.ShapeDtypeStruct((rows, width), jnp.bfloat16),
            jax.ShapeDtypeStruct((local * dims + TILE, width), jnp.bfloat16),
            jax.ShapeDtypeStruct((local, 128), jnp.int32),
        ),
        in_specs=[SMEM] + [HBM] * 4,
        out_specs=(VMEM, VMEM, VMEM),
        scratch_shapes=[
            pltpu.VMEM((TILE, width), jnp.float32),
            pltpu.VMEM((local, slots), jnp.int32),
            pltpu.SMEM((local,), jnp.int32),
            pltpu.SemaphoreType.DMA((2 * local + 2,)),
        ],
        compiler_params=pltpu.CompilerParams(vmem_limit_bytes=4 << 20),
        name="pack",
    )(
        first_leaf[None],
        *[
            pltpu.with_memory_space_constraint(a, pltpu.HBM)
            for a in (counts, points, weights, neighbours)
        ],
    )

    order = (1, 3, 2)
    row = {0: target}
    for d in order:
        row[d] = moved(target, d, 1)
    lists = {0: listed}
    for d in order:
        lists[d] = moved(listed, d, 1)
    column = {0: source}
    for d in order:
        column[d] = moved(source, d, 0)
    join = pl.pallas_call(
        join_kernel,
        out_shape=jax.ShapeDtypeStruct((2 * rows, width), jnp.bfloat16),
        in_specs=[VMEM] * 2,
        out_specs=VMEM,
        compiler_params=pltpu.CompilerParams(vmem_limit_bytes=4 << 20),
        name="join",
    )
    sides = []
    for ring in (up, down):
        sides.append([lax.ppermute(source, "owner", ring)])
    for d in order[:2]:
        for ring, side in zip((up, down), sides):
            side.append(lax.ppermute(column[d], "owner", ring))

    room = SIDE * local * slots + 8
    me = jnp.stack([helper // SIDE, helper % SIDE]).astype(jnp.int32)
    make_lists = pl.pallas_call(
        functools.partial(list_kernel, slots),
        out_shape=(
            jax.ShapeDtypeStruct((room,), jnp.int32),
            jax.ShapeDtypeStruct((room,), jnp.int32),
        ),
        in_specs=[SMEM] + [VMEM] * SIDE,
        out_specs=(SMEM, SMEM),
        scratch_shapes=[
            pltpu.VMEM((SIDE * local, 128), jnp.int32),
            pltpu.SMEM((SIDE * local, 128), jnp.int32),
            pltpu.SemaphoreType.DMA,
        ],
        compiler_params=pltpu.CompilerParams(vmem_limit_bytes=4 << 20),
        name="lists",
    )
    own, far = make_lists(me, *[lists[d] for d in range(SIDE)])
    row[1], own, far = lax.optimization_barrier((row[1], own, far))
    make_targets = pl.pallas_call(
        target_kernel,
        out_shape=jax.ShapeDtypeStruct((SIDE * local, dims + TILE, width), jnp.bfloat16),
        in_specs=[VMEM] * SIDE,
        out_specs=VMEM,
        scratch_shapes=[
            pltpu.VMEM((TILE, width), jnp.float32),
            pltpu.VMEM((TILE, width), jnp.float32),
        ],
        compiler_params=pltpu.CompilerParams(vmem_limit_bytes=8 << 20),
        name="targets",
    )
    tgt = make_targets(*[row[d] for d in range(SIDE)])
    opposite, tgt, own, far = lax.optimization_barrier((column[2], tgt, own, far))
    for ring, side in zip((up, down), sides):
        side.append(lax.ppermute(opposite, "owner", ring))

    (total,) = pair_sums(
        own,
        [source, column[1], opposite, column[3]],
        tuple((d, 0) for d in range(SIDE)),
        tgt,
        vectors,
    )
    places = []
    for s in range(2):
        places += [(4 * s, 0), (4 * s + 1, 0), (4 * s + 3, 0), (4 * s + 2, 0)]
    parts = pair_sums(far, sides[0] + sides[1], tuple(places), tgt, vectors, total)
    result = parts[0]
    for d in order:
        result = result + moved(parts[d], -d, 1).astype(jnp.float32)
    return result


def solution(mesh):
    placed = (
        P(("owner", "helper"), None, None),
        P(("owner", "helper"), None, None),
        P(("owner", "helper"), None),
        P(("owner", "helper")),
    )
    return jax.shard_map(
        potentials,
        mesh=mesh,
        in_specs=placed,
        out_specs=P(("owner", "helper"), None, None),
        check_vma=False,
    )
```

```python
import functools

import jax
import jax.numpy as jnp
from jax import lax
from jax.experimental import pallas as pl
from jax.experimental.pallas import tpu as pltpu
from jax.sharding import PartitionSpec as P


LOG2E = 1.4426950408889634
SIDE = 4
LOCAL = 4
GROUP = LOCAL * SIDE * SIDE
UNROLL = 8
TAIL = 2
CHUNK = 128
PRE = 128
AT_ONCE = 4
TILE = 16
LISTS = 12
UNUSED = 255


def moved(value, step, along):
    pairs = []
    for h in range(SIDE * SIDE):
        r, c = divmod(h, SIDE)
        if along == 0:
            to = ((r + step) % SIDE) * SIDE + c
        else:
            to = r * SIDE + (c + step) % SIDE
        pairs.append((h, to))
    return lax.ppermute(value, "helper", pairs)


def nn(a, b):
    return lax.dot_general(
        a, b, (((1,), (0,)), ((), ())), preferred_element_type=jnp.float32
    )


def tn(a, b):
    return lax.dot_general(
        a, b, (((0,), (0,)), ((), ())), preferred_element_type=jnp.float32
    )


def pack_kernel(
    first_ref, counts_hbm, points, weights, lists, s_out, t_out, tile, near, counts, sems
):
    dims = points.shape[1]
    vectors = weights.shape[1]
    slots = lists.shape[1]
    top = LOCAL * dims
    copies = []
    for i in range(LOCAL):
        here = s_out.at[i * dims : (i + 1) * dims]
        copies.append(pltpu.make_async_copy(points.at[i], here, sems.at[i]))
    for i in range(LOCAL):
        at = top + TILE + i * vectors
        here = s_out.at[at : at + vectors]
        copies.append(pltpu.make_async_copy(weights.at[i], here, sems.at[LOCAL + i]))
    copies.append(pltpu.make_async_copy(lists, near, sems.at[2 * LOCAL]))
    copies.append(pltpu.make_async_copy(counts_hbm, counts, sems.at[2 * LOCAL + 1]))
    for copy in copies:
        copy.start()
    for i in range(LOCAL):
        copies[i].wait()
        coords = s_out[i * dims : (i + 1) * dims]
        t_out[i * dims : (i + 1) * dims] = coords
        wide = coords.astype(jnp.float32)
        n = jnp.sum(wide * wide, axis=0, keepdims=True)
        high = n.astype(jnp.bfloat16).astype(jnp.float32)
        rest = n - high
        middle = rest.astype(jnp.bfloat16).astype(jnp.float32)
        tile[3 * i : 3 * i + 1] = high
        tile[3 * i + 1 : 3 * i + 2] = middle
        tile[3 * i + 2 : 3 * i + 3] = rest - middle
    tile[LISTS : LISTS + 3] = jnp.ones((3, tile.shape[1]), jnp.float32)
    tile[LISTS + 3 :] = jnp.zeros((1, tile.shape[1]), jnp.float32)
    s_out[top : top + TILE] = tile[...].astype(jnp.bfloat16)
    tile[LISTS:] = jnp.zeros((LOCAL, tile.shape[1]), jnp.float32)
    copies[2 * LOCAL].wait()
    copies[2 * LOCAL + 1].wait()
    slot = lax.broadcasted_iota(jnp.int32, (1, slots), 1)
    for i in range(LOCAL):
        size = counts[i]
        place = jnp.where(slot < size, near[i : i + 1] - first_ref[0], UNUSED)
        tile[LISTS + i : LISTS + i + 1, :slots] = place.astype(jnp.float32)
        tile[LISTS + i : LISTS + i + 1, slots : slots + 1] = jnp.full(
            (1, 1), size, jnp.int32
        ).astype(jnp.float32)
    t_out[top:] = tile[...].astype(jnp.bfloat16)
    for copy in copies[LOCAL : 2 * LOCAL]:
        copy.wait()


def join_kernel(a, b, out):
    rows = a.shape[0]
    out[:rows] = a[...]
    out[rows:] = b[...]


def target_kernel(slots, me_ref, *refs):
    blocks, refs = refs[:SIDE], refs[SIDE:]
    tgt, own_ref, far_ref, tile, norm, keys, keys_s, sem = refs
    dims = tgt.shape[1] - TILE
    top = LOCAL * dims
    norm[...] = jnp.full(norm.shape, -0.5, jnp.float32)
    norm[LISTS + 3 :] = jnp.zeros((1, norm.shape[1]), jnp.float32)
    for b, ref in enumerate(blocks):
        tile[...] = ref[top:].astype(jnp.float32)
        keys[b * LOCAL : (b + 1) * LOCAL] = tile[LISTS:, :128].astype(jnp.int32)
    s = keys[...]
    g, h, i = s >> 6, (s >> 2) & 15, s & 3
    used = s < UNUSED
    lane = lax.broadcasted_iota(jnp.int32, s.shape, 1)
    t = lax.broadcasted_iota(jnp.int32, s.shape, 0)
    block = ((me_ref[0] - (h >> 2)) & 3) * LOCAL + i
    slot = jnp.where(used, block + jnp.where(g == 2, SIDE * LOCAL, 0), 0)
    mine = used & ((h & 3) == me_ref[1])
    kind = jnp.where(mine, jnp.where(g == 1, 1, 2), 0)
    key = (kind << 24) | (t << 16) | (t << 8) | slot
    keys[...] = jnp.where(lane == slots, s, key)
    copy = pltpu.make_async_copy(keys, keys_s, sem)
    copy.start()
    for b, ref in enumerate(blocks):
        tile[...] = ref[top:].astype(jnp.float32)
        for j in range(LOCAL):
            tgt[b * LOCAL + j, :dims] = ref[j * dims : (j + 1) * dims]
            norm[LISTS : LISTS + 3] = -0.5 * tile[3 * j : 3 * j + 3]
            tgt[b * LOCAL + j, dims:] = norm[...].astype(jnp.bfloat16)
    copy.wait()

    def per_target(t, carry):
        def some(q, carry):
            own, far = carry
            for u in range(AT_ONCE):
                key = keys_s[t, AT_ONCE * q + u]
                own_ref[own + 1] = key
                far_ref[far + 1] = key
                own = own + ((key >> 24) & 1)
                far = far + (key >> 25)
            return own, far

        turns = (keys_s[t, slots] + (AT_ONCE - 1)) >> 2
        return lax.fori_loop(0, turns, some, carry)

    targets = SIDE * LOCAL
    own, far = lax.fori_loop(0, targets, per_target, (jnp.int32(0), jnp.int32(0)))
    own_ref[0] = own
    far_ref[0] = far
    for u in range(1, TAIL + 3):
        own_ref[own + u] = jnp.int32(targets << 16)
        far_ref[far + u] = jnp.int32(targets << 16)


def pair_kernel(places, last, keys_ref, *refs):
    n_refs = 1 + max(p[0] for p in places)
    source_refs, refs = refs[:n_refs], refs[n_refs:]
    tgt, refs = refs[0], refs[1:]
    if last:
        start_ref, refs = refs[0], refs[1:]
    out_refs, refs = refs[: SIDE if last else 1], refs[SIDE if last else 1 :]
    src, wts, acc, k0, k1, s0, s1 = refs
    dims = tgt.shape[1] - TILE
    width = tgt.shape[2]
    targets = tgt.shape[0]
    top = LOCAL * dims
    vectors = acc.shape[1]
    kb, sb = (k0, k1), (s0, s1)

    row = lax.broadcasted_iota(jnp.int32, (TILE, width), 0)
    for b, (operand, at) in enumerate(places):
        block = source_refs[operand]
        tile = block[at + top : at + top + TILE].astype(jnp.float32)
        for i in range(LOCAL):
            on = ((row >= 3 * i) & (row < 3 * i + 3)) | (row >= LISTS)
            slot = b * LOCAL + i
            src[slot, :dims] = block[at + i * dims : at + (i + 1) * dims]
            src[slot, dims:] = jnp.where(on, tile, 0.0).astype(jnp.bfloat16)
            first = at + top + TILE + i * vectors
            wts[slot] = block[first : first + vectors]
    if last:
        acc[:targets] = start_ref[...]
    else:
        acc[:targets] = jnp.zeros((targets,) + acc.shape[1:], jnp.float32)
    acc[targets] = jnp.zeros(acc.shape[1:], jnp.float32)
    k1[...] = jnp.zeros_like(k1)

    def picked(p):
        key = keys_ref[p + 1]
        return key & 255, (key >> 8) & 255, (key >> 16) & 255

    def ahead(p, buffer):
        s, t, _ = picked(p)
        rows = tgt[t]
        for lo in range(0, PRE, CHUNK):
            buffer[lo : lo + CHUNK] = tn(src[s, :, lo : lo + CHUNK], rows)

    def gauss(e):
        return jnp.exp2(e * LOG2E).astype(jnp.bfloat16)

    def step(p, k_in, k_out, s_now, s_next):
        s, t, _ = picked(p)
        rows = tgt[t]
        for lo in range(0, PRE, CHUNK):
            k_out[lo : lo + CHUNK] = gauss(s_now[lo : lo + CHUNK])
        for lo in range(PRE, width, CHUNK):
            k_out[lo : lo + CHUNK] = gauss(tn(src[s, :, lo : lo + CHUNK], rows))
        ahead(p + 1, s_next)
        s, _, a = picked(jnp.maximum(p - 1, 0))
        acc[a] += nn(wts[s], k_in[...])

    ahead(0, s0)

    def turn(first, steps):
        for u in range(steps):
            step(
                first + u,
                kb[(u + 1) % 2],
                kb[u % 2],
                sb[u % 2],
                sb[(u + 1) % 2],
            )

    def body(h, carry):
        turn(UNROLL * h, UNROLL)
        return carry

    def tail(h, carry):
        turn(whole + TAIL * h, TAIL)
        return carry

    steps = keys_ref[0] + 1
    turns = steps // UNROLL
    whole = turns * UNROLL
    lax.fori_loop(0, turns, body, 0)
    lax.fori_loop(0, (steps - whole + TAIL - 1) // TAIL, tail, 0)
    if last:
        for d, ref in enumerate(out_refs):
            ref[...] = acc[d * LOCAL : (d + 1) * LOCAL].astype(ref.dtype)
    else:
        out_refs[0][...] = acc[:targets]


SMEM = pl.BlockSpec(memory_space=pltpu.SMEM)
VMEM = pl.BlockSpec(memory_space=pltpu.VMEM)
HBM = pl.BlockSpec(memory_space=pltpu.HBM)


def pair_sums(keys, operands, places, tgt, vectors, start=None):
    targets, deep, width = tgt.shape
    dims = deep - TILE
    rows = LOCAL * (dims + vectors) + TILE
    last = start is not None
    if last:
        part = (LOCAL, vectors, width)
        out = [jax.ShapeDtypeStruct(part, jnp.float32)]
        out += [jax.ShapeDtypeStruct(part, jnp.bfloat16)] * (SIDE - 1)
    else:
        out = [jax.ShapeDtypeStruct((targets, vectors, width), jnp.float32)]
    pairs = 40
    return pl.pallas_call(
        functools.partial(pair_kernel, places, last),
        out_shape=out,
        in_specs=[SMEM] + [VMEM] * (len(operands) + 1 + last),
        out_specs=[VMEM] * len(out),
        scratch_shapes=[
            pltpu.VMEM((len(places) * LOCAL, deep, width), jnp.bfloat16),
            pltpu.VMEM((len(places) * LOCAL, vectors, width), jnp.bfloat16),
            pltpu.VMEM((targets + 1, vectors, width), jnp.float32),
            pltpu.VMEM((width, width), jnp.bfloat16),
            pltpu.VMEM((width, width), jnp.bfloat16),
            pltpu.VMEM((PRE, width), jnp.float32),
            pltpu.VMEM((PRE, width), jnp.float32),
        ],
        compiler_params=pltpu.CompilerParams(vmem_limit_bytes=14 << 20),
        cost_estimate=pl.CostEstimate(
            flops=2 * pairs * width * width * deep,
            transcendentals=pairs * width * width,
            bytes_accessed=len(places) * rows * width * 2,
        ),
        name="pairs_far" if last else "pairs_own",
    )(keys, *operands, tgt, *((start,) if last else ()))


def potentials(points, weights, neighbours, counts):
    local, dims, width = points.shape
    vectors = weights.shape[1]
    slots = neighbours.shape[1]
    owners = lax.axis_size("owner")
    helper = lax.axis_index("helper")
    first_leaf = (lax.axis_index("owner") - 1) * GROUP
    up = [(i, (i + 1) % owners) for i in range(owners)]
    down = [(j, i) for i, j in up]

    rows = local * (dims + vectors) + TILE
    source, target = pl.pallas_call(
        pack_kernel,
        out_shape=(
            jax.ShapeDtypeStruct((rows, width), jnp.bfloat16),
            jax.ShapeDtypeStruct((local * dims + TILE, width), jnp.bfloat16),
        ),
        in_specs=[SMEM] + [HBM] * 4,
        out_specs=(VMEM, VMEM),
        scratch_shapes=[
            pltpu.VMEM((TILE, width), jnp.float32),
            pltpu.VMEM((local, slots), jnp.int32),
            pltpu.SMEM((local,), jnp.int32),
            pltpu.SemaphoreType.DMA((2 * local + 2,)),
        ],
        compiler_params=pltpu.CompilerParams(vmem_limit_bytes=4 << 20),
        name="pack",
    )(
        first_leaf[None],
        *[
            pltpu.with_memory_space_constraint(a, pltpu.HBM)
            for a in (counts, points, weights, neighbours)
        ],
    )

    order = (1, 3, 2)
    row = {0: target}
    for d in order:
        row[d] = moved(target, d, 1)
    column = {0: source}
    for d in order:
        column[d] = moved(source, d, 0)
    join = pl.pallas_call(
        join_kernel,
        out_shape=jax.ShapeDtypeStruct((2 * rows, width), jnp.bfloat16),
        in_specs=[VMEM] * 2,
        out_specs=VMEM,
        compiler_params=pltpu.CompilerParams(vmem_limit_bytes=4 << 20),
        name="join",
    )
    sides = []
    for ring in (up, down):
        sides.append([lax.ppermute(source, "owner", ring)])
    for d in order[:2]:
        for ring, side in zip((up, down), sides):
            side.append(lax.ppermute(column[d], "owner", ring))

    room = SIDE * local * slots + 8
    me = jnp.stack([helper // SIDE, helper % SIDE]).astype(jnp.int32)
    make_targets = pl.pallas_call(
        functools.partial(target_kernel, slots),
        out_shape=(
            jax.ShapeDtypeStruct((SIDE * local, dims + TILE, width), jnp.bfloat16),
            jax.ShapeDtypeStruct((room,), jnp.int32),
            jax.ShapeDtypeStruct((room,), jnp.int32),
        ),
        in_specs=[SMEM] + [VMEM] * SIDE,
        out_specs=(VMEM, SMEM, SMEM),
        scratch_shapes=[
            pltpu.VMEM((TILE, width), jnp.float32),
            pltpu.VMEM((TILE, width), jnp.float32),
            pltpu.VMEM((SIDE * local, 128), jnp.int32),
            pltpu.SMEM((SIDE * local, 128), jnp.int32),
            pltpu.SemaphoreType.DMA,
        ],
        compiler_params=pltpu.CompilerParams(vmem_limit_bytes=8 << 20),
        name="targets",
    )
    tgt, own, far = make_targets(me, *[row[d] for d in range(SIDE)])
    opposite, tgt, own, far = lax.optimization_barrier((column[2], tgt, own, far))
    for ring, side in zip((up, down), sides):
        side.append(lax.ppermute(opposite, "owner", ring))

    (total,) = pair_sums(
        own,
        [source, column[1], opposite, column[3]],
        tuple((d, 0) for d in range(SIDE)),
        tgt,
        vectors,
    )
    places = []
    for s in range(2):
        places += [(4 * s, 0), (4 * s + 1, 0), (4 * s + 3, 0), (4 * s + 2, 0)]
    parts = pair_sums(far, sides[0] + sides[1], tuple(places), tgt, vectors, total)
    result = parts[0]
    for d in order:
        result = result + moved(parts[d], -d, 1).astype(jnp.float32)
    return result


def solution(mesh):
    placed = (
        P(("owner", "helper"), None, None),
        P(("owner", "helper"), None, None),
        P(("owner", "helper"), None),
        P(("owner", "helper")),
    )
    return jax.shard_map(
        potentials,
        mesh=mesh,
        in_specs=placed,
        out_specs=P(("owner", "helper"), None, None),
        check_vma=False,
    )
```
